32 devices in a mesh: groups: 1, rows: 16 (over z, y, core), heads: 2 (over x).
Axes of the slice: x: 2, y: 2, z: 4, core: 2. Of those that a mesh axis runs over, the one named last changes fastest.
Arguments:
- queries: bfloat16 [2048, 8192], P(('groups', 'rows'), 'heads'), may hold values from -40 to 40
- passages: bfloat16 [768, 1024], P(('groups', 'rows')), may hold values from -6 to 6
- enc_gain: bfloat16 [1024], replicated, may hold values from 0.099609375 to 1.8984375
- key_weight: bfloat16 [1024, 8192], P(None, 'heads'), may hold values from -0.1875 to 0.1875
- value_weight: bfloat16 [1024, 8192], P(None, 'heads'), may hold values from -0.1875 to 0.1875
- out_weight: bfloat16 [8192, 1024], P('heads'), may hold values from -0.125 to 0.125
- passage_length: int32 [3], P('groups'), may hold values from 64 to 256, as said below
Outputs:
- cross_out: bfloat16 [2048, 1024], P(('groups', 'rows'))
The draws below stay inside these ranges and needn't reach their ends.
Inputs may be any that keep to these rules, and one draw needn't show every extreme that they name: `passage_length`: every passage has at least a quarter of its padded tokens; some passage is full and some has exactly 64 tokens.
All inputs are finite; a program needn't handle non-finite values.
Results may differ from the reference program's by a relative error of at most 0.012.
The reference program's roundings to bfloat16 on the way count: a program that leaves them out, or rounds other values in their place, can miss the bound.
Values may be sent and summed in bfloat16 or wider, within the bound.
A program may use at most 128 MiB of HBM per device.

```python
import jax
import jax.numpy as jnp
from jax import lax

D = 1024
HEADS = 64
DK = 128
PASS_LEN = 256
ENC = 768
DEC = 2048
PASSAGES = 3


def draw_queries(key, part):
    first = jax.random.fold_in(key, 11)
    shape = (DEC, HEADS * DK)
    base = jnp.clip(0.25 * jax.random.normal(first, shape, jnp.float32), -1.5, 1.5)
    return base.astype(jnp.bfloat16)


def draw_passage_length(key, part):
    first = jax.random.fold_in(key, 21)
    second = jax.random.fold_in(key, 22)
    lowest_len = PASS_LEN // 4
    base = jax.random.randint(first, (PASSAGES,), lowest_len, PASS_LEN + 1)
    order = jax.random.permutation(second, PASSAGES)
    base = base.at[order[0]].set(PASS_LEN)
    base = base.at[order[1]].set(lowest_len)
    return base.astype(jnp.int32)


def steps_of(own_key, shape, pieces, low, top_value):
    factor_of, own = 1.0, jax.random.fold_in(own_key, 6)
    for position, shards_of in pieces:
        draws = jnp.exp(jax.random.uniform(jax.random.fold_in(own, position), (shards_of,), jnp.float32, low / len(pieces), top_value / len(pieces)))
        factor_of = factor_of * jnp.repeat(draws, shape[position] // shards_of).reshape([-1 if axis == position else 1 for axis in range(len(shape))])
    return factor_of


def scatter_about(key, dims, width, most, shards=(), held_as=jnp.bfloat16):
    loudness = steps_of(key, dims, shards, -0.22, 0.18) if shards else 1.0
    values = jax.random.normal(key, dims, jnp.float32) * width * loudness
    return jnp.minimum(jnp.maximum(values, -most), most).astype(held_as)


def setup_inputs(seed: int = 0, part: int = 0) -> dict:
    streams_of = jax.random.split(jax.random.key(seed), 8)
    part_splits = jax.random.split(jax.random.fold_in(streams_of[7], part), 8)
    return {
        "queries": draw_queries(jax.random.fold_in(jax.random.fold_in(streams_of[7], part), 71), part),
        "passages": scatter_about(part_splits[1], (ENC, D), 1.0, 6.0, ((0, 16),)),
        "enc_gain": jnp.clip(1.0 + 0.18 * jax.random.normal(streams_of[2], (D,), jnp.float32), 0.099609375, 1.8984375).astype(jnp.bfloat16),
        "key_weight": scatter_about(streams_of[3], (D, HEADS * DK), D ** -0.5, 0.1875, ((1, 2),)),
        "value_weight": scatter_about(streams_of[4], (D, HEADS * DK), D ** -0.5, 0.1875, ((1, 2),)),
        "out_weight": scatter_about(streams_of[5], (HEADS * DK, D), (HEADS * DK // 4) ** -0.5, 0.125, ((0, 2),)),
        "passage_length": draw_passage_length(jax.random.fold_in(jax.random.fold_in(streams_of[7], part), 71), part),
    }


LOWEST = -1e+30

def normalize(passages, enc_gain):
    wide = passages.astype(jnp.float32)
    mean_square = lax.optimization_barrier(jnp.mean(wide * wide, axis=-1, keepdims=True))
    return (wide * lax.rsqrt(mean_square + 1e-06) * enc_gain.astype(jnp.float32)).astype(jnp.bfloat16)

def reference(queries, passages, enc_gain, key_weight, value_weight, out_weight, passage_length):
    normed = normalize(passages, enc_gain)
    keys = jnp.dot(normed, key_weight, preferred_element_type=jnp.float32).astype(jnp.bfloat16)
    values = jnp.dot(normed, value_weight, preferred_element_type=jnp.float32).astype(jnp.bfloat16)
    positions = jnp.arange(ENC, dtype=jnp.int32)
    owner = positions // PASS_LEN
    valid = positions % PASS_LEN < passage_length[owner]
    key_heads = keys.reshape(ENC, HEADS, DK).transpose(1, 0, 2)
    value_heads = values.reshape(ENC, HEADS, DK).transpose(1, 0, 2)
    query_heads = queries.reshape(DEC, HEADS, DK).transpose(1, 0, 2)

    def one_head(operands):
        query_rows, key_rows, value_rows = operands
        scores = jnp.dot(query_rows, key_rows.T, preferred_element_type=jnp.float32)
        masked = jnp.where(valid[None, :], scores, LOWEST)
        top = lax.optimization_barrier(jnp.max(masked, axis=-1, keepdims=True))
        expo = jnp.where(valid[None, :], jnp.exp(scores - top), 0.0)
        denom = lax.optimization_barrier(jnp.sum(expo, axis=-1, keepdims=True))
        mixed = jnp.dot(expo.astype(jnp.bfloat16), value_rows, preferred_element_type=jnp.float32)
        return (mixed / denom).astype(jnp.bfloat16)
    attended = lax.map(one_head, (query_heads, key_heads, value_heads))
    attended = attended.transpose(1, 0, 2).reshape(DEC, HEADS * DK)
    return jnp.dot(attended, out_weight, preferred_element_type=jnp.float32).astype(jnp.bfloat16)
```

```python
import functools

import jax
import jax.numpy as jnp
from jax import lax
from jax.experimental import pallas as pl
from jax.experimental.pallas import tpu as pltpu
from jax.sharding import PartitionSpec as P

DK = 128
PASS_LEN = 256
SHORT_LEN = PASS_LEN // 4
LOWEST = -1e30
MESH = pl.DeviceIdType.MESH
LOADS = 4
GROUP = 256
OUT_CHUNK = 512
ROW_BLOCK = 16
GIVE, SHARED, REST = 0, 1, 2
SPLITS = 2


def flip(index, bits):
    bit = 1
    while bit <= bits:
        if bits & bit:
            index = index + bit - 2 * bit * ((index // bit) % 2)
        bit *= 2
    return index


def kernel(
    n_rows,
    n_heads,
    length_ref,
    queries_ref,
    passages_ref,
    gain_ref,
    key_ref,
    value_ref,
    outw_ref,
    out_ref,
    own_raw,
    rows,
    query_buf,
    key_w,
    value_w,
    out_w,
    keys,
    values,
    key_sum,
    value_sum,
    score_buf,
    weight_buf,
    attended,
    core_send,
    core_recv,
    own_part,
    x_parts,
    local_sem,
    load_sem,
    send_sem,
    recv_sem,
    query_sem,
    out_core_sem,
    out_x_sem,
):
    block, width = passages_ref.shape
    dec, inner = queries_ref.shape
    half = inner // 2
    n_pass = length_ref.shape[0]
    n_z = n_rows // 4
    quarter = width // 4
    middle = width - 2 * quarter
    bf16 = jnp.bfloat16
    f32 = jnp.float32

    me = lax.axis_index("rows")
    x = lax.axis_index("heads")
    core = me % 2
    y = (me // 2) % 2
    z = me // 4
    side = x % 2

    def at_row(r):
        return {"rows": r}

    partner = at_row(flip(me, 1))
    across_y = at_row(flip(me, 2))
    z_peers = [at_row(flip(me, 4 * d)) for d in range(1, n_z)]
    x_peers = [{"heads": flip(x, d)} for d in range(1, n_heads)]
    across_x = x_peers[0]

    own_rows = pltpu.make_async_copy(passages_ref, own_raw, local_sem.at[0])
    own_rows.start()
    barrier = pltpu.get_barrier_semaphore()
    peers = z_peers + [across_y, partner] + x_peers
    for peer in peers:
        pl.semaphore_signal(barrier, inc=1, device_id=peer, device_id_type=MESH)

    mine = pl.ds(pl.multiple_of(core * half, 128), half)
    theirs = pl.ds(pl.multiple_of((1 - core) * half, 128), half)
    share = half // LOADS
    loads = []
    for part in range(LOADS):
        here = pl.ds(part * share, share)
        there = pl.ds(pl.multiple_of(core * half + part * share, 128), share)
        loads.append(
            (
                pltpu.make_async_copy(
                    key_ref.at[:, there], key_w.at[:, here], load_sem.at[0, part]
                ),
                pltpu.make_async_copy(
                    value_ref.at[:, there], value_w.at[:, here], load_sem.at[1, part]
                ),
                pltpu.make_async_copy(outw_ref.at[there], out_w.at[here], load_sem.at[2, part]),
            )
        )
    own_queries = pltpu.make_async_copy(
        queries_ref.at[:, mine], query_buf.at[0:dec], local_sem.at[1]
    )

    def slot_of(dy, dz):
        return dy * n_z + dz

    def place(slot, c):
        return pl.ds(pl.multiple_of(slot * 2 * block + c * block, 16), block)

    give_at = pl.multiple_of(side * (width - quarter), 128)
    rest_at = pl.multiple_of((1 - side) * (width - quarter), 128)
    main_at = pl.multiple_of(side * quarter, 128)
    main_cols = pl.ds(main_at, width - quarter)
    rest_cols = pl.ds(rest_at, quarter)
    cols_of = {GIVE: pl.ds(give_at, quarter), SHARED: pl.ds(quarter, middle), REST: rest_cols}

    def unit_of(slot, c, kind):
        return rows.at[place(slot, c), cols_of[kind]]

    def whole_of(slot, c):
        return rows.at[place(slot, c)]

    own_rows.wait()
    for triple in loads:
        triple[0].start()
        triple[1].start()
    own_queries.start()
    for triple in loads:
        triple[2].start()
    wide_rows = own_raw[...].astype(f32)
    mean_square = jnp.mean(wide_rows * wide_rows, axis=-1, keepdims=True)
    gain = gain_ref[...].astype(f32).reshape(1, width)
    rows[place(0, core), :] = (wide_rows * lax.rsqrt(mean_square + 1e-06) * gain).astype(bf16)

    pl.semaphore_wait(barrier, len(peers))

    sent = []

    def send(src, dst, send_at, recv_at, to):
        copy = pltpu.make_async_remote_copy(
            src_ref=src, dst_ref=dst, send_sem=send_at, recv_sem=recv_at,
            device_id=to, device_id_type=MESH,
        )
        copy.start()
        sent.append(copy)

    count = [0]

    def next_sem():
        count[0] += 1
        return send_sem.at[count[0] - 1]

    def send_unit(slot, kind, to, there_slot, there_kind):
        send(
            unit_of(slot, core, kind),
            unit_of(there_slot, core, kind),
            next_sem(),
            recv_sem.at[there_slot, core, there_kind],
            to,
        )

    def await_unit(slot, c, kind):
        view = unit_of(slot, c, kind)
        pltpu.make_async_copy(view, view, recv_sem.at[slot, c, kind]).wait()

    for kind in (GIVE, SHARED):
        for d in range(n_z - 1, 0, -1):
            send_unit(0, kind, z_peers[d - 1], slot_of(0, d), kind)
        send_unit(0, kind, across_y, slot_of(1, 0), kind)
    send(whole_of(0, core), whole_of(0, core), next_sem(), recv_sem.at[0, core, 0], partner)
    send(
        queries_ref.at[:, theirs], query_buf.at[dec : 2 * dec], query_sem.at[0], query_sem.at[1], partner
    )

    def relay(slot, kind, over_y):
        await_unit(slot, core, kind)
        if over_y:
            send_unit(slot, kind, across_y, slot + n_z, kind)
        if kind == GIVE:
            send_unit(slot, kind, across_x, slot, REST)
        send_unit(slot, kind, partner, slot, kind)

    groups = half // GROUP
    waited = set()

    def weights_for(g):
        part = g * GROUP // share
        if part not in waited:
            waited.add(part)
            loads[part][0].wait()
            loads[part][1].wait()

    def keep(slots, cols, made_keys, made_values):
        made_keys = made_keys.astype(bf16)
        made_values = made_values.astype(bf16)
        for number, slot in enumerate(slots):
            dy, dz = slot // n_z, slot % n_z
            chip = flip(z, dz) * 2 + flip(y, dy)
            to = pl.ds(pl.multiple_of(chip * 2 * block, 16), 2 * block)
            part = slice(number * 2 * block, (number + 1) * 2 * block)
            keys[to, cols] = made_keys[part]
            values[to, cols] = made_values[part]

    def rows_in(slots):
        return slice(slots[0] * 2 * block, (slots[-1] + 1) * 2 * block)

    def project(slots, g):
        weights_for(g)
        cols = slice(g * GROUP, (g + 1) * GROUP)
        chunk = rows[rows_in(slots), :]
        keep(
            slots,
            cols,
            jnp.dot(chunk, key_w[:, cols], preferred_element_type=f32),
            jnp.dot(chunk, value_w[:, cols], preferred_element_type=f32),
        )

    def project_main(slots, g):
        cols = slice(g * GROUP, (g + 1) * GROUP)
        chunk = rows[rows_in(slots), main_cols]
        here = slice(0, len(slots) * 2 * block)
        key_sum[here, cols] = jnp.dot(chunk, key_w[main_cols, cols], preferred_element_type=f32)
        value_sum[here, cols] = jnp.dot(chunk, value_w[main_cols, cols], preferred_element_type=f32)

    def project_rest(slots, g):
        cols = slice(g * GROUP, (g + 1) * GROUP)
        chunk = rows[rows_in(slots), rest_cols]
        here = slice(0, len(slots) * 2 * block)
        keep(
            slots,
            cols,
            key_sum[here, cols]
            + jnp.dot(chunk, key_w[rest_cols, cols], preferred_element_type=f32),
            value_sum[here, cols]
            + jnp.dot(chunk, value_w[rest_cols, cols], preferred_element_type=f32),
        )

    def interleave(pieces, events, each):
        events = list(events)
        for piece in pieces:
            piece()
            for event in events[:each]:
                event()
            events = events[each:]
        for event in events:
            event()

    def pieces_of(work, slots):
        return [functools.partial(work, slots, g) for g in range(groups)]

    near = list(range(n_z - 1, 0, -1))
    line = [slot_of(0, d) for d in near]
    other = [slot_of(1, d) for d in near]
    beside = slot_of(1, 0)

    def from_partner(slots, kinds):
        for slot in slots:
            for kind in kinds:
                await_unit(slot, 1 - core, kind)

    R = functools.partial
    relay(beside, GIVE, False)
    view = whole_of(0, 1 - core)
    pltpu.make_async_copy(view, view, recv_sem.at[0, 1 - core, 0]).wait()
    events = [R(relay, beside, SHARED, False)]
    events += [R(relay, s, GIVE, True) for s in line]
    events += [R(relay, beside, REST, False)]
    events += [R(relay, s, SHARED, True) for s in line]
    interleave(pieces_of(project, [0]), events, 1)
    from_partner([beside], (GIVE, SHARED, REST))
    events = []
    for s, o in zip(line, other):
        events += [R(relay, o, GIVE, False), R(relay, s, REST, False)]
    interleave(pieces_of(project, [beside]), events, 2)
    from_partner(line, (GIVE, SHARED, REST))
    events = [R(relay, o, SHARED, False) for o in other]
    events += [R(relay, o, REST, False) for o in other]
    interleave(pieces_of(project, line[::-1]), events, 1)
    from_partner(other, (GIVE, SHARED))
    interleave(pieces_of(project_main, other[::-1]), [], 1)
    from_partner(other, (REST,))
    for piece in pieces_of(project_rest, other[::-1]):
        piece()

    lengths = [length_ref[p] for p in range(n_pass)]
    short_at = jnp.int32(0)
    full_at = jnp.int32(0)
    short_open = jnp.int32(1)
    full_open = jnp.int32(1)
    for p in range(n_pass):
        hit = short_open * (lengths[p] == SHORT_LEN).astype(jnp.int32)
        short_at = short_at + hit * p
        short_open = short_open - hit
        hit = full_open * (lengths[p] == PASS_LEN).astype(jnp.int32)
        full_at = full_at + hit * p
        full_open = full_open - hit
    starts = [full_at]
    tails = []
    for j in range(n_pass - 2):
        low = short_at + (full_at < short_at).astype(jnp.int32) * (full_at - short_at)
        high = short_at + full_at - low
        at = j + (j >= low).astype(jnp.int32)
        at = at + (at >= high).astype(jnp.int32)
        starts.append(at)
        length = jnp.int32(0)
        for p in range(n_pass):
            length = length + (at == p).astype(jnp.int32) * lengths[p]
        offsets = lax.broadcasted_iota(jnp.int32, (1, PASS_LEN), 1)
        tails.append(jnp.where(offsets < length, 0.0, LOWEST).astype(f32))
    starts = [at * PASS_LEN for at in starts]
    short_start = short_at * PASS_LEN
    kept = (n_pass - 1) * PASS_LEN + SHORT_LEN
    number = kept + SHORT_LEN

    own_queries.wait()
    view = query_buf.at[dec : 2 * dec]
    pltpu.make_async_copy(view, view, query_sem.at[1]).wait()

    heads = half // DK
    counted = jnp.concatenate(
        [jnp.ones((kept, DK), bf16), jnp.zeros((SHORT_LEN, DK), bf16)], axis=0
    )

    def head_cols(h):
        return slice(h * DK, (h + 1) * DK)

    def score(h, low, high):
        cols = head_cols(h)
        asked = jnp.concatenate([query_buf[low:high, cols], query_buf[dec + low : dec + high, cols]], axis=0)
        last = keys[pl.ds(short_start, SHORT_LEN), cols]
        against = jnp.concatenate(
            [keys[pl.ds(at, PASS_LEN), cols] for at in starts] + [last, last], axis=0
        )
        score_buf[h % 2] = lax.dot_general(
            asked, against, (((1,), (1,)), ((), ())), preferred_element_type=f32
        )

    def weigh(h, low, high):
        for row in range(0, 2 * (high - low), ROW_BLOCK):
            here = slice(row, row + ROW_BLOCK)
            scores = score_buf[h % 2, here, :]
            scores = jnp.concatenate(
                [scores[:, :PASS_LEN]]
                + [
                    scores[:, (j + 1) * PASS_LEN : (j + 2) * PASS_LEN] + tails[j]
                    for j in range(n_pass - 2)
                ]
                + [scores[:, (n_pass - 1) * PASS_LEN :]],
                axis=1,
            )
            top = jnp.max(scores, axis=-1, keepdims=True)
            weight_buf[h % 2, here, :] = jnp.exp(scores - top).astype(bf16)

    def mix(h, low, high):
        cols = head_cols(h)
        size = high - low
        taken = jnp.concatenate(
            [values[pl.ds(at, PASS_LEN), cols] for at in starts]
            + [values[pl.ds(short_start, SHORT_LEN), cols], jnp.zeros((SHORT_LEN, DK), bf16)],
            axis=0,
        )
        taken = jnp.concatenate([taken, counted], axis=1)
        mixed = jnp.dot(weight_buf[h % 2], taken, preferred_element_type=f32)
        mixed = (mixed[:, :DK] / mixed[:, DK:]).astype(bf16)
        attended[low:high, cols] = mixed[:size]
        attended[dec + low : dec + high, cols] = mixed[size:]

    def attend(low, high, hooks):
        for step in range(heads + 2):
            if step < heads:
                score(step, low, high)
            if 0 < step < heads + 1:
                weigh(step - 1, low, high)
            if 1 < step:
                mix(step - 2, low, high)
            if step in hooks:
                hooks[step]()

    chunks = width // OUT_CHUNK

    def chunk_of(j):
        return slice(j * OUT_CHUNK, (j + 1) * OUT_CHUNK)

    def to_core(n, low, high):
        here = slice(low, high)
        size = high - low
        mixed = jnp.concatenate([attended[low:high, :], attended[dec + low : dec + high, :]], axis=0)
        for j in range(chunks):
            cols = chunk_of(j)
            made = jnp.dot(mixed, out_w[:, cols], preferred_element_type=f32)
            core_send[here, cols] = made[size:].astype(bf16)
            send(
                core_send.at[here, cols], core_recv.at[here, cols], out_core_sem.at[0, n, j],
                out_core_sem.at[1, n, j], partner,
            )
            own_part[here, cols] = made[:size]

    def to_x(n, low, high):
        here = slice(low, high)
        for j in range(chunks):
            cols = chunk_of(j)
            view = core_recv.at[here, cols]
            pltpu.make_async_copy(view, view, out_core_sem.at[1, n, j]).wait()
            x_parts[x, here, cols] = (
                own_part[here, cols] + core_recv[here, cols].astype(f32)
            ).astype(bf16)
            view = x_parts.at[x, here, cols]
            for d, peer in enumerate(x_peers):
                send(view, view, out_x_sem.at[0, n, d, j], out_x_sem.at[1, n, d, j], peer)

    def finish(n, low, high):
        here = slice(low, high)
        for j in range(chunks):
            cols = chunk_of(j)
            for d in range(1, n_heads):
                view = x_parts.at[flip(x, d), here, cols]
                pltpu.make_async_copy(view, view, out_x_sem.at[1, n, d - 1, j]).wait()
            total = x_parts[0, here, cols].astype(f32)
            for term in range(1, n_heads):
                total += x_parts[term, here, cols].astype(f32)
            out_ref[here, cols] = total.astype(bf16)

    size = dec // SPLITS
    bounds = [(n * size, (n + 1) * size) for n in range(SPLITS)]
    for n, (low, high) in enumerate(bounds):
        hooks = {}
        if n:
            hooks[5] = functools.partial(to_x, n - 1, *bounds[n - 1])
        attend(low, high, hooks)
        if not n:
            for triple in loads:
                triple[2].wait()
        to_core(n, low, high)
    to_x(SPLITS - 1, *bounds[-1])
    for n, (low, high) in enumerate(bounds):
        finish(n, low, high)
    for copy in sent:
        copy.wait_send()


def on_device(
    n_rows, n_heads, queries, passages, enc_gain, key_weight, value_weight, out_weight, passage_length
):
    dec, inner = queries.shape
    block, width = passages.shape
    half = inner // 2
    n_pass = passage_length.shape[0]
    number = (n_pass - 1) * PASS_LEN + 2 * SHORT_LEN
    n_z = n_rows // 4
    slots = 2 * n_z
    chunks = width // OUT_CHUNK
    bf16 = jnp.bfloat16
    dma = pltpu.SemaphoreType.DMA
    vmem = pl.BlockSpec(memory_space=pltpu.VMEM)
    anywhere = pl.BlockSpec(memory_space=pl.ANY)
    n_sends = 2 * (n_z - 1) + 2 * n_z + 1 + (slots - 1) + 3 * (slots - 1)
    return pl.pallas_call(
        functools.partial(kernel, n_rows, n_heads),
        out_shape=jax.ShapeDtypeStruct((dec, width), bf16),
        in_specs=[
            pl.BlockSpec(memory_space=pltpu.SMEM),
            anywhere,
            anywhere,
            vmem,
            anywhere,
            anywhere,
            anywhere,
        ],
        out_specs=vmem,
        scratch_shapes=[
            pltpu.VMEM((block, width), bf16),
            pltpu.VMEM((n_rows * block, width), bf16),
            pltpu.VMEM((2 * dec, half), bf16),
            pltpu.VMEM((width, half), bf16),
            pltpu.VMEM((width, half), bf16),
            pltpu.VMEM((half, width), bf16),
            pltpu.VMEM((n_rows * block, half), bf16),
            pltpu.VMEM((n_rows * block, half), bf16),
            pltpu.VMEM(((n_z - 1) * 2 * block, half), jnp.float32),
            pltpu.VMEM(((n_z - 1) * 2 * block, half), jnp.float32),
            pltpu.VMEM((2, 2 * dec // SPLITS, number), jnp.float32),
            pltpu.VMEM((2, 2 * dec // SPLITS, number), bf16),
            pltpu.VMEM((2 * dec, half), bf16),
            pltpu.VMEM((dec, width), bf16),
            pltpu.VMEM((dec, width), bf16),
            pltpu.VMEM((dec, width), jnp.float32),
            pltpu.VMEM((n_heads, dec, width), bf16),
            dma((2,)),
            dma((3, LOADS)),
            dma((n_sends,)),
            dma((slots, 2, 3)),
            dma((2,)),
            dma((2, SPLITS, chunks)),
            dma((2, SPLITS, n_heads - 1, chunks)),
        ],
        compiler_params=pltpu.CompilerParams(
            collective_id=0, has_side_effects=True, vmem_limit_bytes=40 * 1024 * 1024
        ),
    )(
        *(
            pltpu.with_memory_space_constraint(array, pltpu.HBM)
            for array in (
                passage_length,
                queries,
                passages,
                enc_gain,
                key_weight,
                value_weight,
                out_weight,
            )
        )
    )


def solution(mesh):
    return jax.shard_map(
        functools.partial(on_device, mesh.shape["rows"], mesh.shape["heads"]),
        mesh=mesh,
        in_specs=(
            P(("groups", "rows"), "heads"),
            P(("groups", "rows"), None),
            P(),
            P(None, "heads"),
            P(None, "heads"),
            P("heads", None),
            P("groups"),
        ),
        out_specs=P(("groups", "rows"), None),
        check_vma=False,
    )
```

```python
import functools

import jax
import jax.numpy as jnp
from jax import lax
from jax.experimental import pallas as pl
from jax.experimental.pallas import tpu as pltpu
from jax.sharding import PartitionSpec as P

DK = 128
PASS_LEN = 256
SHORT_LEN = PASS_LEN // 4
LOWEST = -1e30
MESH = pl.DeviceIdType.MESH
LOADS = 4
GROUP = 256
OUT_CHUNK = 512
ROW_BLOCK = 16
GIVE, SHARED, REST = 0, 1, 2
SPLITS = 2
PARTS = (2, 2, 1)
EACH = (3, 2, 3)


def flip(index, bits):
    bit = 1
    while bit <= bits:
        if bits & bit:
            index = index + bit - 2 * bit * ((index // bit) % 2)
        bit *= 2
    return index


def kernel(
    n_rows,
    n_heads,
    length_ref,
    queries_ref,
    passages_ref,
    gain_ref,
    key_ref,
    value_ref,
    outw_ref,
    out_ref,
    own_raw,
    rows,
    query_buf,
    key_w,
    value_w,
    out_w,
    keys,
    values,
    key_sum,
    value_sum,
    score_buf,
    weight_buf,
    attended,
    core_send,
    core_recv,
    own_part,
    x_parts,
    local_sem,
    load_sem,
    send_sem,
    recv_sem,
    query_sem,
    out_core_sem,
    out_x_sem,
):
    block, width = passages_ref.shape
    dec, inner = queries_ref.shape
    half = inner // 2
    n_pass = length_ref.shape[0]
    n_z = n_rows // 4
    quarter = width // 4
    middle = width - 2 * quarter
    bf16 = jnp.bfloat16
    f32 = jnp.float32

    me = lax.axis_index("rows")
    x = lax.axis_index("heads")
    core = me % 2
    y = (me // 2) % 2
    z = me // 4
    side = x % 2

    def at_row(r):
        return {"rows": r}

    partner = at_row(flip(me, 1))
    across_y = at_row(flip(me, 2))
    z_peers = [at_row(flip(me, 4 * d)) for d in range(1, n_z)]
    x_peers = [{"heads": flip(x, d)} for d in range(1, n_heads)]
    across_x = x_peers[0]

    own_rows = pltpu.make_async_copy(passages_ref, own_raw, local_sem.at[0])
    own_rows.start()
    barrier = pltpu.get_barrier_semaphore()
    peers = z_peers + [across_y, partner] + x_peers
    for peer in peers:
        pl.semaphore_signal(barrier, inc=1, device_id=peer, device_id_type=MESH)

    mine = pl.ds(pl.multiple_of(core * half, 128), half)
    theirs = pl.ds(pl.multiple_of((1 - core) * half, 128), half)
    share = half // LOADS
    loads = []
    for part in range(LOADS):
        here = pl.ds(part * share, share)
        there = pl.ds(pl.multiple_of(core * half + part * share, 128), share)
        loads.append(
            (
                pltpu.make_async_copy(
                    key_ref.at[:, there], key_w.at[:, here], load_sem.at[0, part]
                ),
                pltpu.make_async_copy(
                    value_ref.at[:, there], value_w.at[:, here], load_sem.at[1, part]
                ),
                pltpu.make_async_copy(outw_ref.at[there], out_w.at[here], load_sem.at[2, part]),
            )
        )
    own_queries = pltpu.make_async_copy(
        queries_ref.at[:, mine], query_buf.at[0:dec], local_sem.at[1]
    )

    def slot_of(dy, dz):
        return dy * n_z + dz

    def place(slot, c):
        return pl.ds(pl.multiple_of(slot * 2 * block + c * block, 16), block)

    give_at = pl.multiple_of(side * (width - quarter), 128)
    rest_at = pl.multiple_of((1 - side) * (width - quarter), 128)
    main_at = pl.multiple_of(side * quarter, 128)
    main_cols = pl.ds(main_at, width - quarter)
    rest_cols = pl.ds(rest_at, quarter)
    cols_of = {GIVE: pl.ds(give_at, quarter), SHARED: pl.ds(quarter, middle), REST: rest_cols}

    def unit_of(slot, c, kind):
        return rows.at[place(slot, c), cols_of[kind]]

    def whole_of(slot, c):
        return rows.at[place(slot, c)]

    own_rows.wait()
    for triple in loads:
        triple[0].start()
        triple[1].start()
    own_queries.start()
    for triple in loads:
        triple[2].start()
    wide_rows = own_raw[...].astype(f32)
    mean_square = jnp.mean(wide_rows * wide_rows, axis=-1, keepdims=True)
    gain = gain_ref[...].astype(f32).reshape(1, width)
    rows[place(0, core), :] = (wide_rows * lax.rsqrt(mean_square + 1e-06) * gain).astype(bf16)

    pl.semaphore_wait(barrier, len(peers))

    sent = []

    def send(src, dst, send_at, recv_at, to):
        copy = pltpu.make_async_remote_copy(
            src_ref=src, dst_ref=dst, send_sem=send_at, recv_sem=recv_at,
            device_id=to, device_id_type=MESH,
        )
        copy.start()
        sent.append(copy)

    count = [0]

    def next_sem():
        count[0] += 1
        return send_sem.at[count[0] - 1]

    def send_unit(slot, kind, to, there_slot, there_kind):
        send(
            unit_of(slot, core, kind),
            unit_of(there_slot, core, kind),
            next_sem(),
            recv_sem.at[there_slot, core, there_kind],
            to,
        )

    def await_unit(slot, c, kind):
        view = unit_of(slot, c, kind)
        pltpu.make_async_copy(view, view, recv_sem.at[slot, c, kind]).wait()

    def send_own(kind):
        for d in range(n_z - 1, 0, -1):
            send_unit(0, kind, z_peers[d - 1], slot_of(0, d), kind)
        send_unit(0, kind, across_y, slot_of(1, 0), kind)

    send_own(GIVE)
    send(whole_of(0, core), whole_of(0, core), next_sem(), recv_sem.at[0, core, 0], partner)
    send(
        queries_ref.at[:, theirs], query_buf.at[dec : 2 * dec], query_sem.at[0], query_sem.at[1], partner
    )

    def relay(slot, kind, over_y):
        await_unit(slot, core, kind)
        if over_y:
            send_unit(slot, kind, across_y, slot + n_z, kind)
        if kind == GIVE:
            send_unit(slot, kind, across_x, slot, REST)
        send_unit(slot, kind, partner, slot, kind)

    groups = half // GROUP
    waited = set()

    def weights_for(g):
        part = g * GROUP // share
        if part not in waited:
            waited.add(part)
            loads[part][0].wait()
            loads[part][1].wait()

    def keep(slots, cols, made_keys, made_values):
        made_keys = made_keys.astype(bf16)
        made_values = made_values.astype(bf16)
        for number, slot in enumerate(slots):
            dy, dz = slot // n_z, slot % n_z
            chip = flip(z, dz) * 2 + flip(y, dy)
            to = pl.ds(pl.multiple_of(chip * 2 * block, 16), 2 * block)
            part = slice(number * 2 * block, (number + 1) * 2 * block)
            keys[to, cols] = made_keys[part]
            values[to, cols] = made_values[part]

    def rows_in(slots):
        return slice(slots[0] * 2 * block, (slots[-1] + 1) * 2 * block)

    def project(slots, g):
        weights_for(g)
        cols = slice(g * GROUP, (g + 1) * GROUP)
        chunk = rows[rows_in(slots), :]
        keep(
            slots,
            cols,
            jnp.dot(chunk, key_w[:, cols], preferred_element_type=f32),
            jnp.dot(chunk, value_w[:, cols], preferred_element_type=f32),
        )

    def project_main(slots, g):
        cols = slice(g * GROUP, (g + 1) * GROUP)
        chunk = rows[rows_in(slots), main_cols]
        here = slice(0, len(slots) * 2 * block)
        key_sum[here, cols] = jnp.dot(chunk, key_w[main_cols, cols], preferred_element_type=f32)
        value_sum[here, cols] = jnp.dot(chunk, value_w[main_cols, cols], preferred_element_type=f32)

    def project_rest(slots, g):
        cols = slice(g * GROUP, (g + 1) * GROUP)
        chunk = rows[rows_in(slots), rest_cols]
        here = slice(0, len(slots) * 2 * block)
        keep(
            slots,
            cols,
            key_sum[here, cols]
            + jnp.dot(chunk, key_w[rest_cols, cols], preferred_element_type=f32),
            value_sum[here, cols]
            + jnp.dot(chunk, value_w[rest_cols, cols], preferred_element_type=f32),
        )

    def interleave(pieces, events, each):
        events = list(events)
        for piece in pieces:
            piece()
            for event in events[:each]:
                event()
            events = events[each:]
        for event in events:
            event()

    def pieces_of(work, slots, parts):
        def piece(part):
            for g in range(groups * part // parts, groups * (part + 1) // parts):
                work(slots, g)

        return [functools.partial(piece, part) for part in range(parts)]

    near = list(range(n_z - 1, 0, -1))
    line = [slot_of(0, d) for d in near]
    other = [slot_of(1, d) for d in near]
    beside = slot_of(1, 0)

    def from_partner(slots, kinds):
        for slot in slots:
            for kind in kinds:
                await_unit(slot, 1 - core, kind)

    R = functools.partial
    view = whole_of(0, 1 - core)
    pltpu.make_async_copy(view, view, recv_sem.at[0, 1 - core, 0]).wait()
    interleave(pieces_of(project, [0], 2), [R(send_own, SHARED)], 1)
    relay(beside, GIVE, False)
    for s in line:
        relay(s, GIVE, True)
    relay(beside, SHARED, False)
    relay(beside, REST, False)
    for s in line:
        relay(s, SHARED, True)
    from_partner([beside], (GIVE, SHARED, REST))
    events = []
    for s, o in zip(line, other):
        events += [R(relay, o, GIVE, False), R(relay, s, REST, False)]
    interleave(pieces_of(project, [beside], PARTS[0]), events, EACH[0])
    from_partner(line, (GIVE, SHARED))
    events = [R(relay, o, SHARED, False) for o in other]
    interleave(pieces_of(project_main, line[::-1], PARTS[1]), events, EACH[1])
    from_partner(line, (REST,))
    events = [R(relay, o, REST, False) for o in other]
    interleave(pieces_of(project_rest, line[::-1], PARTS[2]), events, EACH[2])
    from_partner(other, (GIVE, SHARED))
    interleave(pieces_of(project_main, other[::-1], 1), [], 1)
    from_partner(other, (REST,))
    interleave(pieces_of(project_rest, other[::-1], 1), [], 1)

    lengths = [length_ref[p] for p in range(n_pass)]
    short_at = jnp.int32(0)
    full_at = jnp.int32(0)
    short_open = jnp.int32(1)
    full_open = jnp.int32(1)
    for p in range(n_pass):
        hit = short_open * (lengths[p] == SHORT_LEN).astype(jnp.int32)
        short_at = short_at + hit * p
        short_open = short_open - hit
        hit = full_open * (lengths[p] == PASS_LEN).astype(jnp.int32)
        full_at = full_at + hit * p
        full_open = full_open - hit
    starts = [full_at]
    tails = []
    for j in range(n_pass - 2):
        low = short_at + (full_at < short_at).astype(jnp.int32) * (full_at - short_at)
        high = short_at + full_at - low
        at = j + (j >= low).astype(jnp.int32)
        at = at + (at >= high).astype(jnp.int32)
        starts.append(at)
        length = jnp.int32(0)
        for p in range(n_pass):
            length = length + (at == p).astype(jnp.int32) * lengths[p]
        offsets = lax.broadcasted_iota(jnp.int32, (1, PASS_LEN), 1)
        tails.append(jnp.where(offsets < length, 0.0, LOWEST).astype(f32))
    starts = [at * PASS_LEN for at in starts]
    short_start = short_at * PASS_LEN
    kept = (n_pass - 1) * PASS_LEN + SHORT_LEN
    number = kept + SHORT_LEN

    own_queries.wait()
    view = query_buf.at[dec : 2 * dec]
    pltpu.make_async_copy(view, view, query_sem.at[1]).wait()

    heads = half // DK
    counted = jnp.concatenate(
        [jnp.ones((kept, DK), bf16), jnp.zeros((SHORT_LEN, DK), bf16)], axis=0
    )

    def head_cols(h):
        return slice(h * DK, (h + 1) * DK)

    def score(h, low, high):
        cols = head_cols(h)
        asked = jnp.concatenate([query_buf[low:high, cols], query_buf[dec + low : dec + high, cols]], axis=0)
        last = keys[pl.ds(short_start, SHORT_LEN), cols]
        against = jnp.concatenate(
            [keys[pl.ds(at, PASS_LEN), cols] for at in starts] + [last, last], axis=0
        )
        score_buf[h % 2] = lax.dot_general(
            asked, against, (((1,), (1,)), ((), ())), preferred_element_type=f32
        )

    def weigh(h, low, high):
        for row in range(0, 2 * (high - low), ROW_BLOCK):
            here = slice(row, row + ROW_BLOCK)
            scores = score_buf[h % 2, here, :]
            scores = jnp.concatenate(
                [scores[:, :PASS_LEN]]
                + [
                    scores[:, (j + 1) * PASS_LEN : (j + 2) * PASS_LEN] + tails[j]
                    for j in range(n_pass - 2)
                ]
                + [scores[:, (n_pass - 1) * PASS_LEN :]],
                axis=1,
            )
            top = jnp.max(scores, axis=-1, keepdims=True)
            weight_buf[h % 2, here, :] = jnp.exp(scores - top).astype(bf16)

    def mix(h, low, high):
        cols = head_cols(h)
        size = high - low
        taken = jnp.concatenate(
            [values[pl.ds(at, PASS_LEN), cols] for at in starts]
            + [values[pl.ds(short_start, SHORT_LEN), cols], jnp.zeros((SHORT_LEN, DK), bf16)],
            axis=0,
        )
        taken = jnp.concatenate([taken, counted], axis=1)
        mixed = jnp.dot(weight_buf[h % 2], taken, preferred_element_type=f32)
        mixed = (mixed[:, :DK] / mixed[:, DK:]).astype(bf16)
        attended[low:high, cols] = mixed[:size]
        attended[dec + low : dec + high, cols] = mixed[size:]

    def attend(low, high, hooks):
        for step in range(heads + 2):
            if step < heads:
                score(step, low, high)
            if 0 < step < heads + 1:
                weigh(step - 1, low, high)
            if 1 < step:
                mix(step - 2, low, high)
            if step in hooks:
                hooks[step]()

    chunks = width // OUT_CHUNK

    def chunk_of(j):
        return slice(j * OUT_CHUNK, (j + 1) * OUT_CHUNK)

    def to_core(n, low, high):
        here = slice(low, high)
        size = high - low
        mixed = jnp.concatenate([attended[low:high, :], attended[dec + low : dec + high, :]], axis=0)
        for j in range(chunks):
            cols = chunk_of(j)
            made = jnp.dot(mixed, out_w[:, cols], preferred_element_type=f32)
            core_send[here, cols] = made[size:].astype(bf16)
            send(
                core_send.at[here, cols], core_recv.at[here, cols], out_core_sem.at[0, n, j],
                out_core_sem.at[1, n, j], partner,
            )
            own_part[here, cols] = made[:size]

    def to_x(n, low, high):
        here = slice(low, high)
        for j in range(chunks):
            cols = chunk_of(j)
            view = core_recv.at[here, cols]
            pltpu.make_async_copy(view, view, out_core_sem.at[1, n, j]).wait()
            x_parts[x, here, cols] = (
                own_part[here, cols] + core_recv[here, cols].astype(f32)
            ).astype(bf16)
            view = x_parts.at[x, here, cols]
            for d, peer in enumerate(x_peers):
                send(view, view, out_x_sem.at[0, n, d, j], out_x_sem.at[1, n, d, j], peer)

    def finish(n, low, high):
        here = slice(low, high)
        for j in range(chunks):
            cols = chunk_of(j)
            for d in range(1, n_heads):
                view = x_parts.at[flip(x, d), here, cols]
                pltpu.make_async_copy(view, view, out_x_sem.at[1, n, d - 1, j]).wait()
            total = x_parts[0, here, cols].astype(f32)
            for term in range(1, n_heads):
                total += x_parts[term, here, cols].astype(f32)
            out_ref[here, cols] = total.astype(bf16)

    size = dec // SPLITS
    bounds = [(n * size, (n + 1) * size) for n in range(SPLITS)]
    for n, (low, high) in enumerate(bounds):
        hooks = {}
        if n:
            hooks[5] = functools.partial(to_x, n - 1, *bounds[n - 1])
        attend(low, high, hooks)
        if not n:
            for triple in loads:
                triple[2].wait()
        to_core(n, low, high)
    to_x(SPLITS - 1, *bounds[-1])
    for n, (low, high) in enumerate(bounds):
        finish(n, low, high)
    for copy in sent:
        copy.wait_send()


def on_device(
    n_rows, n_heads, queries, passages, enc_gain, key_weight, value_weight, out_weight, passage_length
):
    dec, inner = queries.shape
    block, width = passages.shape
    half = inner // 2
    n_pass = passage_length.shape[0]
    number = (n_pass - 1) * PASS_LEN + 2 * SHORT_LEN
    n_z = n_rows // 4
    slots = 2 * n_z
    chunks = width // OUT_CHUNK
    bf16 = jnp.bfloat16
    dma = pltpu.SemaphoreType.DMA
    vmem = pl.BlockSpec(memory_space=pltpu.VMEM)
    anywhere = pl.BlockSpec(memory_space=pl.ANY)
    n_sends = 2 * (n_z - 1) + 2 * n_z + 1 + (slots - 1) + 3 * (slots - 1)
    return pl.pallas_call(
        functools.partial(kernel, n_rows, n_heads),
        out_shape=jax.ShapeDtypeStruct((dec, width), bf16),
        in_specs=[
            pl.BlockSpec(memory_space=pltpu.SMEM),
            anywhere,
            anywhere,
            vmem,
            anywhere,
            anywhere,
            anywhere,
        ],
        out_specs=vmem,
        scratch_shapes=[
            pltpu.VMEM((block, width), bf16),
            pltpu.VMEM((n_rows * block, width), bf16),
            pltpu.VMEM((2 * dec, half), bf16),
            pltpu.VMEM((width, half), bf16),
            pltpu.VMEM((width, half), bf16),
            pltpu.VMEM((half, width), bf16),
            pltpu.VMEM((n_rows * block, half), bf16),
            pltpu.VMEM((n_rows * block, half), bf16),
            pltpu.VMEM(((n_z - 1) * 2 * block, half), jnp.float32),
            pltpu.VMEM(((n_z - 1) * 2 * block, half), jnp.float32),
            pltpu.VMEM((2, 2 * dec // SPLITS, number), jnp.float32),
            pltpu.VMEM((2, 2 * dec // SPLITS, number), bf16),
            pltpu.VMEM((2 * dec, half), bf16),
            pltpu.VMEM((dec, width), bf16),
            pltpu.VMEM((dec, width), bf16),
            pltpu.VMEM((dec, width), jnp.float32),
            pltpu.VMEM((n_heads, dec, width), bf16),
            dma((2,)),
            dma((3, LOADS)),
            dma((n_sends,)),
            dma((slots, 2, 3)),
            dma((2,)),
            dma((2, SPLITS, chunks)),
            dma((2, SPLITS, n_heads - 1, chunks)),
        ],
        compiler_params=pltpu.CompilerParams(
            collective_id=0, has_side_effects=True, vmem_limit_bytes=40 * 1024 * 1024
        ),
    )(
        *(
            pltpu.with_memory_space_constraint(array, pltpu.HBM)
            for array in (
                passage_length,
                queries,
                passages,
                enc_gain,
                key_weight,
                value_weight,
                out_weight,
            )
        )
    )


def solution(mesh):
    return jax.shard_map(
        functools.partial(on_device, mesh.shape["rows"], mesh.shape["heads"]),
        mesh=mesh,
        in_specs=(
            P(("groups", "rows"), "heads"),
            P(("groups", "rows"), None),
            P(),
            P(None, "heads"),
            P(None, "heads"),
            P("heads", None),
            P("groups"),
        ),
        out_specs=P(("groups", "rows"), None),
        check_vma=False,
    )
```

```python
import functools

import jax
import jax.numpy as jnp
from jax import lax
from jax.experimental import pallas as pl
from jax.experimental.pallas import tpu as pltpu
from jax.sharding import PartitionSpec as P

DK = 128
PASS_LEN = 256
SHORT_LEN = PASS_LEN // 4
LOWEST = -1e30
MESH = pl.DeviceIdType.MESH
LOADS = 4
GROUP = 256
OUT_CHUNK = 512
ROW_BLOCK = 16
GIVE, SHARED, REST = 0, 1, 2
SPLITS = 2
PARTS = 2
EACH = 3


def flip(index, bits):
    bit = 1
    while bit <= bits:
        if bits & bit:
            index = index + bit - 2 * bit * ((index // bit) % 2)
        bit *= 2
    return index


def kernel(
    n_rows,
    n_heads,
    length_ref,
    queries_ref,
    passages_ref,
    gain_ref,
    key_ref,
    value_ref,
    outw_ref,
    out_ref,
    own_raw,
    rows,
    query_buf,
    key_w,
    value_w,
    out_w,
    keys,
    values,
    key_sum,
    value_sum,
    score_buf,
    weight_buf,
    attended,
    core_send,
    core_recv,
    own_part,
    x_parts,
    local_sem,
    load_sem,
    send_sem,
    recv_sem,
    query_sem,
    out_core_sem,
    out_x_sem,
):
    block, width = passages_ref.shape
    dec, inner = queries_ref.shape
    half = inner // 2
    n_pass = length_ref.shape[0]
    n_z = n_rows // 4
    quarter = width // 4
    middle = width - 2 * quarter
    bf16 = jnp.bfloat16
    f32 = jnp.float32

    me = lax.axis_index("rows")
    x = lax.axis_index("heads")
    core = me % 2
    y = (me // 2) % 2
    z = me // 4
    side = x % 2

    def at_row(r):
        return {"rows": r}

    partner = at_row(flip(me, 1))
    across_y = at_row(flip(me, 2))
    z_peers = [at_row(flip(me, 4 * d)) for d in range(1, n_z)]
    x_peers = [{"heads": flip(x, d)} for d in range(1, n_heads)]
    across_x = x_peers[0]

    own_rows = pltpu.make_async_copy(passages_ref, own_raw, local_sem.at[0])
    own_rows.start()
    barrier = pltpu.get_barrier_semaphore()
    peers = z_peers + [across_y, partner] + x_peers
    for peer in peers:
        pl.semaphore_signal(barrier, inc=1, device_id=peer, device_id_type=MESH)

    mine = pl.ds(pl.multiple_of(core * half, 128), half)
    theirs = pl.ds(pl.multiple_of((1 - core) * half, 128), half)
    share = half // LOADS
    loads = []
    for part in range(LOADS):
        here = pl.ds(part * share, share)
        there = pl.ds(pl.multiple_of(core * half + part * share, 128), share)
        loads.append(
            (
                pltpu.make_async_copy(
                    key_ref.at[:, there], key_w.at[:, here], load_sem.at[0, part]
                ),
                pltpu.make_async_copy(
                    value_ref.at[:, there], value_w.at[:, here], load_sem.at[1, part]
                ),
                pltpu.make_async_copy(outw_ref.at[there], out_w.at[here], load_sem.at[2, part]),
            )
        )
    own_queries = pltpu.make_async_copy(
        queries_ref.at[:, mine], query_buf.at[0:dec], local_sem.at[1]
    )

    def slot_of(dy, dz):
        return dy * n_z + dz

    def place(slot, c):
        return pl.ds(pl.multiple_of(slot * 2 * block + c * block, 16), block)

    give_at = pl.multiple_of(side * (width - quarter), 128)
    rest_at = pl.multiple_of((1 - side) * (width - quarter), 128)
    rest_cols = pl.ds(rest_at, quarter)
    cols_of = {GIVE: pl.ds(give_at, quarter), SHARED: pl.ds(quarter, middle), REST: rest_cols}

    def unit_of(slot, c, kind):
        return rows.at[place(slot, c), cols_of[kind]]

    def whole_of(slot, c):
        return rows.at[place(slot, c)]

    own_rows.wait()
    for triple in loads:
        triple[0].start()
        triple[1].start()
    own_queries.start()
    for triple in loads:
        triple[2].start()
    wide_rows = own_raw[...].astype(f32)
    mean_square = jnp.mean(wide_rows * wide_rows, axis=-1, keepdims=True)
    gain = gain_ref[...].astype(f32).reshape(1, width)
    rows[place(0, core), :] = (wide_rows * lax.rsqrt(mean_square + 1e-06) * gain).astype(bf16)

    pl.semaphore_wait(barrier, len(peers))

    sent = []

    def send(src, dst, send_at, recv_at, to):
        copy = pltpu.make_async_remote_copy(
            src_ref=src, dst_ref=dst, send_sem=send_at, recv_sem=recv_at,
            device_id=to, device_id_type=MESH,
        )
        copy.start()
        sent.append(copy)

    count = [0]

    def next_sem():
        count[0] += 1
        return send_sem.at[count[0] - 1]

    def send_unit(slot, kind, to, there_slot, there_kind):
        send(
            unit_of(slot, core, kind),
            unit_of(there_slot, core, kind),
            next_sem(),
            recv_sem.at[there_slot, core, there_kind],
            to,
        )

    def await_unit(slot, c, kind):
        view = unit_of(slot, c, kind)
        pltpu.make_async_copy(view, view, recv_sem.at[slot, c, kind]).wait()

    def send_own(kind):
        for d in range(n_z - 1, 0, -1):
            send_unit(0, kind, z_peers[d - 1], slot_of(0, d), kind)
        if kind == GIVE:
            for early in (GIVE, SHARED):
                send_unit(0, early, across_y, slot_of(1, 0), early)

    send_own(GIVE)
    send(whole_of(0, core), whole_of(0, core), next_sem(), recv_sem.at[0, core, 0], partner)
    send(
        queries_ref.at[:, theirs], query_buf.at[dec : 2 * dec], query_sem.at[0], query_sem.at[1], partner
    )

    def relay(slot, kind, over_y):
        await_unit(slot, core, kind)
        if over_y:
            send_unit(slot, kind, across_y, slot + n_z, kind)
        if kind == GIVE:
            send_unit(slot, kind, across_x, slot, REST)
        send_unit(slot, kind, partner, slot, kind)

    groups = half // GROUP
    waited = set()

    def weights_for(g):
        part = g * GROUP // share
        if part not in waited:
            waited.add(part)
            loads[part][0].wait()
            loads[part][1].wait()

    def keep(slots, cols, made_keys, made_values):
        made_keys = made_keys.astype(bf16)
        made_values = made_values.astype(bf16)
        for number, slot in enumerate(slots):
            dy, dz = slot // n_z, slot % n_z
            chip = flip(z, dz) * 2 + flip(y, dy)
            to = pl.ds(pl.multiple_of(chip * 2 * block, 16), 2 * block)
            part = slice(number * 2 * block, (number + 1) * 2 * block)
            keys[to, cols] = made_keys[part]
            values[to, cols] = made_values[part]

    def rows_in(slots):
        return slice(slots[0] * 2 * block, (slots[-1] + 1) * 2 * block)

    def project(slots, g):
        weights_for(g)
        cols = slice(g * GROUP, (g + 1) * GROUP)
        chunk = rows[rows_in(slots), :]
        keep(
            slots,
            cols,
            jnp.dot(chunk, key_w[:, cols], preferred_element_type=f32),
            jnp.dot(chunk, value_w[:, cols], preferred_element_type=f32),
        )

    def project_part(which, cols_in, first, last, slots, g):
        cols = slice(g * GROUP, (g + 1) * GROUP)
        chunk = rows[rows_in(slots), cols_in]
        here = slice(0, len(slots) * 2 * block)
        made_keys = jnp.dot(chunk, key_w[cols_in, cols], preferred_element_type=f32)
        made_values = jnp.dot(chunk, value_w[cols_in, cols], preferred_element_type=f32)
        if not first:
            made_keys += key_sum[which, here, cols]
            made_values += value_sum[which, here, cols]
        if last:
            keep(slots, cols, made_keys, made_values)
        else:
            key_sum[which, here, cols] = made_keys
            value_sum[which, here, cols] = made_values

    def interleave(pieces, events, each):
        events = list(events)
        for piece in pieces:
            piece()
            for event in events[:each]:
                event()
            events = events[each:]
        for event in events:
            event()

    def pieces_of(work, slots, parts):
        def piece(part):
            for g in range(groups * part // parts, groups * (part + 1) // parts):
                work(slots, g)

        return [functools.partial(piece, part) for part in range(parts)]

    near = list(range(n_z - 1, 0, -1))
    line = [slot_of(0, d) for d in near]
    other = [slot_of(1, d) for d in near]
    beside = slot_of(1, 0)

    def from_partner(slots, kinds):
        for slot in slots:
            for kind in kinds:
                await_unit(slot, 1 - core, kind)

    R = functools.partial
    view = whole_of(0, 1 - core)
    pltpu.make_async_copy(view, view, recv_sem.at[0, 1 - core, 0]).wait()
    interleave(pieces_of(project, [0], 2), [R(send_own, SHARED)], 1)
    ahead, across = line[::-1], other[::-1]
    main_cols = pl.ds(pl.multiple_of(side * quarter, 128), width - quarter)
    late_cols = pl.ds(pl.multiple_of((1 - side) * quarter, 128), width - quarter)
    relay(beside, GIVE, False)
    for s in line:
        relay(s, GIVE, True)
    relay(beside, SHARED, False)
    from_partner(line, (GIVE,))
    interleave(pieces_of(R(project_part, 0, cols_of[GIVE], True, False), ahead, 1), [], 1)
    from_partner([beside], (GIVE, SHARED))
    interleave(pieces_of(R(project_part, 1, main_cols, True, False), [beside], 1), [], 1)
    for o in other:
        relay(o, GIVE, False)
    relay(beside, REST, False)
    for s in line:
        relay(s, SHARED, True)
    for s in line:
        relay(s, REST, False)
    from_partner([beside], (REST,))
    interleave(pieces_of(R(project_part, 1, cols_of[REST], False, True), [beside], 1), [], 1)
    from_partner(other, (GIVE,))
    interleave(pieces_of(R(project_part, 1, cols_of[GIVE], True, False), across, 1), [], 1)
    from_partner(line, (SHARED, REST))
    events = [R(relay, o, REST, False) for o in other]
    events += [R(relay, o, SHARED, False) for o in other]
    interleave(pieces_of(R(project_part, 0, late_cols, False, True), ahead, PARTS), events, EACH)
    from_partner(other, (REST,))
    interleave(pieces_of(R(project_part, 1, cols_of[REST], False, False), across, 1), [], 1)
    from_partner(other, (SHARED,))
    interleave(pieces_of(R(project_part, 1, cols_of[SHARED], False, True), across, 1), [], 1)

    lengths = [length_ref[p] for p in range(n_pass)]
    short_at = jnp.int32(0)
    full_at = jnp.int32(0)
    short_open = jnp.int32(1)
    full_open = jnp.int32(1)
    for p in range(n_pass):
        hit = short_open * (lengths[p] == SHORT_LEN).astype(jnp.int32)
        short_at = short_at + hit * p
        short_open = short_open - hit
        hit = full_open * (lengths[p] == PASS_LEN).astype(jnp.int32)
        full_at = full_at + hit * p
        full_open = full_open - hit
    starts = [full_at]
    tails = []
    for j in range(n_pass - 2):
        low = short_at + (full_at < short_at).astype(jnp.int32) * (full_at - short_at)
        high = short_at + full_at - low
        at = j + (j >= low).astype(jnp.int32)
        at = at + (at >= high).astype(jnp.int32)
        starts.append(at)
        length = jnp.int32(0)
        for p in range(n_pass):
            length = length + (at == p).astype(jnp.int32) * lengths[p]
        offsets = lax.broadcasted_iota(jnp.int32, (1, PASS_LEN), 1)
        tails.append(jnp.where(offsets < length, 0.0, LOWEST).astype(f32))
    starts = [at * PASS_LEN for at in starts]
    short_start = short_at * PASS_LEN
    kept = (n_pass - 1) * PASS_LEN + SHORT_LEN
    number = kept + SHORT_LEN

    own_queries.wait()
    view = query_buf.at[dec : 2 * dec]
    pltpu.make_async_copy(view, view, query_sem.at[1]).wait()

    heads = half // DK
    counted = jnp.concatenate(
        [jnp.ones((kept, DK), bf16), jnp.zeros((SHORT_LEN, DK), bf16)], axis=0
    )

    def head_cols(h):
        return slice(h * DK, (h + 1) * DK)

    def score(h, low, high):
        cols = head_cols(h)
        asked = jnp.concatenate([query_buf[low:high, cols], query_buf[dec + low : dec + high, cols]], axis=0)
        last = keys[pl.ds(short_start, SHORT_LEN), cols]
        against = jnp.concatenate(
            [keys[pl.ds(at, PASS_LEN), cols] for at in starts] + [last, last], axis=0
        )
        score_buf[h % 2] = lax.dot_general(
            asked, against, (((1,), (1,)), ((), ())), preferred_element_type=f32
        )

    def weigh(h, low, high):
        for row in range(0, 2 * (high - low), ROW_BLOCK):
            here = slice(row, row + ROW_BLOCK)
            scores = score_buf[h % 2, here, :]
            scores = jnp.concatenate(
                [scores[:, :PASS_LEN]]
                + [
                    scores[:, (j + 1) * PASS_LEN : (j + 2) * PASS_LEN] + tails[j]
                    for j in range(n_pass - 2)
                ]
                + [scores[:, (n_pass - 1) * PASS_LEN :]],
                axis=1,
            )
            top = jnp.max(scores, axis=-1, keepdims=True)
            weight_buf[h % 2, here, :] = jnp.exp(scores - top).astype(bf16)

    def mix(h, low, high):
        cols = head_cols(h)
        size = high - low
        taken = jnp.concatenate(
            [values[pl.ds(at, PASS_LEN), cols] for at in starts]
            + [values[pl.ds(short_start, SHORT_LEN), cols], jnp.zeros((SHORT_LEN, DK), bf16)],
            axis=0,
        )
        taken = jnp.concatenate([taken, counted], axis=1)
        mixed = jnp.dot(weight_buf[h % 2], taken, preferred_element_type=f32)
        mixed = (mixed[:, :DK] / mixed[:, DK:]).astype(bf16)
        attended[low:high, cols] = mixed[:size]
        attended[dec + low : dec + high, cols] = mixed[size:]

    def attend(low, high, hooks):
        for step in range(heads + 2):
            if step < heads:
                score(step, low, high)
            if 0 < step < heads + 1:
                weigh(step - 1, low, high)
            if 1 < step:
                mix(step - 2, low, high)
            if step in hooks:
                hooks[step]()

    chunks = width // OUT_CHUNK

    def chunk_of(j):
        return slice(j * OUT_CHUNK, (j + 1) * OUT_CHUNK)

    def to_core(n, low, high):
        here = slice(low, high)
        size = high - low
        mixed = jnp.concatenate([attended[low:high, :], attended[dec + low : dec + high, :]], axis=0)
        for j in range(chunks):
            cols = chunk_of(j)
            made = jnp.dot(mixed, out_w[:, cols], preferred_element_type=f32)
            core_send[here, cols] = made[size:].astype(bf16)
            send(
                core_send.at[here, cols], core_recv.at[here, cols], out_core_sem.at[0, n, j],
                out_core_sem.at[1, n, j], partner,
            )
            own_part[here, cols] = made[:size]

    def to_x(n, low, high):
        here = slice(low, high)
        for j in range(chunks):
            cols = chunk_of(j)
            view = core_recv.at[here, cols]
            pltpu.make_async_copy(view, view, out_core_sem.at[1, n, j]).wait()
            x_parts[x, here, cols] = (
                own_part[here, cols] + core_recv[here, cols].astype(f32)
            ).astype(bf16)
            view = x_parts.at[x, here, cols]
            for d, peer in enumerate(x_peers):
                send(view, view, out_x_sem.at[0, n, d, j], out_x_sem.at[1, n, d, j], peer)

    def finish(n, low, high):
        here = slice(low, high)
        for j in range(chunks):
            cols = chunk_of(j)
            for d in range(1, n_heads):
                view = x_parts.at[flip(x, d), here, cols]
                pltpu.make_async_copy(view, view, out_x_sem.at[1, n, d - 1, j]).wait()
            total = x_parts[0, here, cols].astype(f32)
            for term in range(1, n_heads):
                total += x_parts[term, here, cols].astype(f32)
            out_ref[here, cols] = total.astype(bf16)

    size = dec // SPLITS
    bounds = [(n * size, (n + 1) * size) for n in range(SPLITS)]
    for n, (low, high) in enumerate(bounds):
        hooks = {}
        if n:
            hooks[5] = functools.partial(to_x, n - 1, *bounds[n - 1])
        attend(low, high, hooks)
        if not n:
            for triple in loads:
                triple[2].wait()
        to_core(n, low, high)
    to_x(SPLITS - 1, *bounds[-1])
    for n, (low, high) in enumerate(bounds):
        finish(n, low, high)
    for copy in sent:
        copy.wait_send()


def on_device(
    n_rows, n_heads, queries, passages, enc_gain, key_weight, value_weight, out_weight, passage_length
):
    dec, inner = queries.shape
    block, width = passages.shape
    half = inner // 2
    n_pass = passage_length.shape[0]
    number = (n_pass - 1) * PASS_LEN + 2 * SHORT_LEN
    n_z = n_rows // 4
    slots = 2 * n_z
    chunks = width // OUT_CHUNK
    bf16 = jnp.bfloat16
    dma = pltpu.SemaphoreType.DMA
    vmem = pl.BlockSpec(memory_space=pltpu.VMEM)
    anywhere = pl.BlockSpec(memory_space=pl.ANY)
    n_sends = 2 * (n_z - 1) + 2 * n_z + 1 + (slots - 1) + 3 * (slots - 1)
    return pl.pallas_call(
        functools.partial(kernel, n_rows, n_heads),
        out_shape=jax.ShapeDtypeStruct((dec, width), bf16),
        in_specs=[
            pl.BlockSpec(memory_space=pltpu.SMEM),
            anywhere,
            anywhere,
            vmem,
            anywhere,
            anywhere,
            anywhere,
        ],
        out_specs=vmem,
        scratch_shapes=[
            pltpu.VMEM((block, width), bf16),
            pltpu.VMEM((n_rows * block, width), bf16),
            pltpu.VMEM((2 * dec, half), bf16),
            pltpu.VMEM((width, half), bf16),
            pltpu.VMEM((width, half), bf16),
            pltpu.VMEM((half, width), bf16),
            pltpu.VMEM((n_rows * block, half), bf16),
            pltpu.VMEM((n_rows * block, half), bf16),
            pltpu.VMEM((2, (n_z - 1) * 2 * block, half), jnp.float32),
            pltpu.VMEM((2, (n_z - 1) * 2 * block, half), jnp.float32),
            pltpu.VMEM((2, 2 * dec // SPLITS, number), jnp.float32),
            pltpu.VMEM((2, 2 * dec // SPLITS, number), bf16),
            pltpu.VMEM((2 * dec, half), bf16),
            pltpu.VMEM((dec, width), bf16),
            pltpu.VMEM((dec, width), bf16),
            pltpu.VMEM((dec, width), jnp.float32),
            pltpu.VMEM((n_heads, dec, width), bf16),
            dma((2,)),
            dma((3, LOADS)),
            dma((n_sends,)),
            dma((slots, 2, 3)),
            dma((2,)),
            dma((2, SPLITS, chunks)),
            dma((2, SPLITS, n_heads - 1, chunks)),
        ],
        compiler_params=pltpu.CompilerParams(
            collective_id=0, has_side_effects=True, vmem_limit_bytes=40 * 1024 * 1024
        ),
    )(
        *(
            pltpu.with_memory_space_constraint(array, pltpu.HBM)
            for array in (
                passage_length,
                queries,
                passages,
                enc_gain,
                key_weight,
                value_weight,
                out_weight,
            )
        )
    )


def solution(mesh):
    return jax.shard_map(
        functools.partial(on_device, mesh.shape["rows"], mesh.shape["heads"]),
        mesh=mesh,
        in_specs=(
            P(("groups", "rows"), "heads"),
            P(("groups", "rows"), None),
            P(),
            P(None, "heads"),
            P(None, "heads"),
            P("heads", None),
            P("groups"),
        ),
        out_specs=P(("groups", "rows"), None),
        check_vma=False,
    )
```

```python
import functools

import jax
import jax.numpy as jnp
from jax import lax
from jax.experimental import pallas as pl
from jax.experimental.pallas import tpu as pltpu
from jax.sharding import PartitionSpec as P

DK = 128
PASS_LEN = 256
SHORT_LEN = PASS_LEN // 4
LOWEST = -1e30
MESH = pl.DeviceIdType.MESH
LOADS = 4
GROUP = 256
OUT_CHUNK = 512
ROW_BLOCK = 16
GIVE, SHARED, REST = 0, 1, 2
SPLITS = 2
PARTS = 2
EACH = 3


def flip(index, bits):
    bit = 1
    while bit <= bits:
        if bits & bit:
            index = index + bit - 2 * bit * ((index // bit) % 2)
        bit *= 2
    return index


def kernel(
    n_rows,
    n_heads,
    length_hbm,
    queries_ref,
    passages_ref,
    gain_hbm,
    key_ref,
    value_ref,
    outw_ref,
    out_ref,
    length_ref,
    gain_ref,
    own_raw,
    rows,
    query_buf,
    key_w,
    value_w,
    out_w,
    keys,
    values,
    key_sum,
    value_sum,
    score_buf,
    weight_buf,
    attended,
    core_send,
    core_recv,
    own_part,
    x_parts,
    local_sem,
    load_sem,
    send_sem,
    recv_sem,
    query_sem,
    out_core_sem,
    out_x_sem,
):
    block, width = passages_ref.shape
    dec, inner = queries_ref.shape
    half = inner // 2
    n_pass = length_ref.shape[0]
    n_z = n_rows // 4
    quarter = width // 4
    middle = width - 2 * quarter
    bf16 = jnp.bfloat16
    f32 = jnp.float32

    me = lax.axis_index("rows")
    x = lax.axis_index("heads")
    core = me % 2
    y = (me // 2) % 2
    z = me // 4
    side = x % 2

    def at_row(r):
        return {"rows": r}

    partner = at_row(flip(me, 1))
    across_y = at_row(flip(me, 2))
    z_peers = [at_row(flip(me, 4 * d)) for d in range(1, n_z)]
    x_peers = [{"heads": flip(x, d)} for d in range(1, n_heads)]
    across_x = x_peers[0]

    own_rows = pltpu.make_async_copy(passages_ref, own_raw, local_sem.at[0])
    own_rows.start()
    own_gain = pltpu.make_async_copy(gain_hbm, gain_ref, local_sem.at[2])
    own_gain.start()
    own_length = pltpu.make_async_copy(length_hbm, length_ref, local_sem.at[3])
    own_length.start()
    barrier = pltpu.get_barrier_semaphore()
    peers = z_peers + [across_y, partner] + x_peers
    for peer in peers:
        pl.semaphore_signal(barrier, inc=1, device_id=peer, device_id_type=MESH)

    mine = pl.ds(pl.multiple_of(core * half, 128), half)
    theirs = pl.ds(pl.multiple_of((1 - core) * half, 128), half)
    share = half // LOADS
    loads = []
    for part in range(LOADS):
        here = pl.ds(part * share, share)
        there = pl.ds(pl.multiple_of(core * half + part * share, 128), share)
        loads.append(
            (
                pltpu.make_async_copy(
                    key_ref.at[:, there], key_w.at[:, here], load_sem.at[0, part]
                ),
                pltpu.make_async_copy(
                    value_ref.at[:, there], value_w.at[:, here], load_sem.at[1, part]
                ),
                pltpu.make_async_copy(outw_ref.at[there], out_w.at[here], load_sem.at[2, part]),
            )
        )
    own_queries = pltpu.make_async_copy(
        queries_ref.at[:, mine], query_buf.at[0:dec], local_sem.at[1]
    )

    def slot_of(dy, dz):
        return dy * n_z + dz

    def place(slot, c):
        return pl.ds(pl.multiple_of(slot * 2 * block + c * block, 16), block)

    give_at = pl.multiple_of(side * (width - quarter), 128)
    rest_at = pl.multiple_of((1 - side) * (width - quarter), 128)
    rest_cols = pl.ds(rest_at, quarter)
    cols_of = {GIVE: pl.ds(give_at, quarter), SHARED: pl.ds(quarter, middle), REST: rest_cols}

    def unit_of(slot, c, kind):
        return rows.at[place(slot, c), cols_of[kind]]

    def whole_of(slot, c):
        return rows.at[place(slot, c)]

    own_rows.wait()
    own_gain.wait()
    for triple in loads:
        triple[0].start()
        triple[1].start()
    own_queries.start()
    for triple in loads:
        triple[2].start()
    wide_rows = own_raw[...].astype(f32)
    mean_square = jnp.mean(wide_rows * wide_rows, axis=-1, keepdims=True)
    gain = gain_ref[...].astype(f32).reshape(1, width)
    rows[place(0, core), :] = (wide_rows * lax.rsqrt(mean_square + 1e-06) * gain).astype(bf16)

    pl.semaphore_wait(barrier, len(peers))

    sent = []

    def send(src, dst, send_at, recv_at, to):
        copy = pltpu.make_async_remote_copy(
            src_ref=src, dst_ref=dst, send_sem=send_at, recv_sem=recv_at,
            device_id=to, device_id_type=MESH,
        )
        copy.start()
        sent.append(copy)

    count = [0]

    def next_sem():
        count[0] += 1
        return send_sem.at[count[0] - 1]

    def send_unit(slot, kind, to, there_slot, there_kind):
        send(
            unit_of(slot, core, kind),
            unit_of(there_slot, core, kind),
            next_sem(),
            recv_sem.at[there_slot, core, there_kind],
            to,
        )

    def await_unit(slot, c, kind):
        view = unit_of(slot, c, kind)
        pltpu.make_async_copy(view, view, recv_sem.at[slot, c, kind]).wait()

    def send_own(kind):
        for d in range(n_z - 1, 0, -1):
            send_unit(0, kind, z_peers[d - 1], slot_of(0, d), kind)
        if kind == GIVE:
            for early in (GIVE, SHARED):
                send_unit(0, early, across_y, slot_of(1, 0), early)

    send_own(GIVE)
    send(whole_of(0, core), whole_of(0, core), next_sem(), recv_sem.at[0, core, 0], partner)
    send(
        queries_ref.at[:, theirs], query_buf.at[dec : 2 * dec], query_sem.at[0], query_sem.at[1], partner
    )

    def relay(slot, kind, over_y):
        await_unit(slot, core, kind)
        if over_y:
            send_unit(slot, kind, across_y, slot + n_z, kind)
        if kind == GIVE:
            send_unit(slot, kind, across_x, slot, REST)
        send_unit(slot, kind, partner, slot, kind)

    groups = half // GROUP
    waited = set()

    def weights_for(g):
        part = g * GROUP // share
        if part not in waited:
            waited.add(part)
            loads[part][0].wait()
            loads[part][1].wait()

    def keep(slots, cols, made_keys, made_values):
        made_keys = made_keys.astype(bf16)
        made_values = made_values.astype(bf16)
        for number, slot in enumerate(slots):
            dy, dz = slot // n_z, slot % n_z
            chip = flip(z, dz) * 2 + flip(y, dy)
            to = pl.ds(pl.multiple_of(chip * 2 * block, 16), 2 * block)
            part = slice(number * 2 * block, (number + 1) * 2 * block)
            keys[to, cols] = made_keys[part]
            values[to, cols] = made_values[part]

    def rows_in(slots):
        return slice(slots[0] * 2 * block, (slots[-1] + 1) * 2 * block)

    def project(slots, g):
        weights_for(g)
        cols = slice(g * GROUP, (g + 1) * GROUP)
        chunk = rows[rows_in(slots), :]
        keep(
            slots,
            cols,
            jnp.dot(chunk, key_w[:, cols], preferred_element_type=f32),
            jnp.dot(chunk, value_w[:, cols], preferred_element_type=f32),
        )

    def project_part(which, cols_in, first, last, slots, g):
        cols = slice(g * GROUP, (g + 1) * GROUP)
        chunk = rows[rows_in(slots), cols_in]
        here = slice(0, len(slots) * 2 * block)
        made_keys = jnp.dot(chunk, key_w[cols_in, cols], preferred_element_type=f32)
        made_values = jnp.dot(chunk, value_w[cols_in, cols], preferred_element_type=f32)
        if not first:
            made_keys += key_sum[which, here, cols]
            made_values += value_sum[which, here, cols]
        if last:
            keep(slots, cols, made_keys, made_values)
        else:
            key_sum[which, here, cols] = made_keys
            value_sum[which, here, cols] = made_values

    def interleave(pieces, events, each):
        events = list(events)
        for piece in pieces:
            piece()
            for event in events[:each]:
                event()
            events = events[each:]
        for event in events:
            event()

    def pieces_of(work, slots, parts):
        def piece(part):
            for g in range(groups * part // parts, groups * (part + 1) // parts):
                work(slots, g)

        return [functools.partial(piece, part) for part in range(parts)]

    near = list(range(n_z - 1, 0, -1))
    line = [slot_of(0, d) for d in near]
    other = [slot_of(1, d) for d in near]
    beside = slot_of(1, 0)

    def from_partner(slots, kinds):
        for slot in slots:
            for kind in kinds:
                await_unit(slot, 1 - core, kind)

    R = functools.partial
    view = whole_of(0, 1 - core)
    pltpu.make_async_copy(view, view, recv_sem.at[0, 1 - core, 0]).wait()
    interleave(pieces_of(project, [0], 2), [R(send_own, SHARED)], 1)
    ahead, across = line[::-1], other[::-1]
    main_cols = pl.ds(pl.multiple_of(side * quarter, 128), width - quarter)
    late_cols = pl.ds(pl.multiple_of((1 - side) * quarter, 128), width - quarter)
    relay(beside, GIVE, False)
    for s in line:
        relay(s, GIVE, True)
    relay(beside, SHARED, False)
    from_partner(line, (GIVE,))
    interleave(pieces_of(R(project_part, 0, cols_of[GIVE], True, False), ahead, 1), [], 1)
    from_partner([beside], (GIVE, SHARED))
    interleave(pieces_of(R(project_part, 1, main_cols, True, False), [beside], 1), [], 1)
    for o in other:
        relay(o, GIVE, False)
    relay(beside, REST, False)
    for s in line:
        relay(s, SHARED, True)
    for s in line:
        relay(s, REST, False)
    from_partner([beside], (REST,))
    interleave(pieces_of(R(project_part, 1, cols_of[REST], False, True), [beside], 1), [], 1)
    from_partner(other, (GIVE,))
    interleave(pieces_of(R(project_part, 1, cols_of[GIVE], True, False), across, 1), [], 1)
    from_partner(line, (SHARED, REST))
    events = [R(relay, o, REST, False) for o in other]
    events += [R(relay, o, SHARED, False) for o in other]
    interleave(pieces_of(R(project_part, 0, late_cols, False, True), ahead, PARTS), events, EACH)
    from_partner(other, (REST,))
    interleave(pieces_of(R(project_part, 1, cols_of[REST], False, False), across, 1), [], 1)
    from_partner(other, (SHARED,))
    interleave(pieces_of(R(project_part, 1, cols_of[SHARED], False, True), across, 1), [], 1)

    own_length.wait()
    lengths = [length_ref[p] for p in range(n_pass)]
    short_at = jnp.int32(0)
    full_at = jnp.int32(0)
    short_open = jnp.int32(1)
    full_open = jnp.int32(1)
    for p in range(n_pass):
        hit = short_open * (lengths[p] == SHORT_LEN).astype(jnp.int32)
        short_at = short_at + hit * p
        short_open = short_open - hit
        hit = full_open * (lengths[p] == PASS_LEN).astype(jnp.int32)
        full_at = full_at + hit * p
        full_open = full_open - hit
    starts = [full_at]
    tails = []
    for j in range(n_pass - 2):
        low = short_at + (full_at < short_at).astype(jnp.int32) * (full_at - short_at)
        high = short_at + full_at - low
        at = j + (j >= low).astype(jnp.int32)
        at = at + (at >= high).astype(jnp.int32)
        starts.append(at)
        length = jnp.int32(0)
        for p in range(n_pass):
            length = length + (at == p).astype(jnp.int32) * lengths[p]
        offsets = lax.broadcasted_iota(jnp.int32, (1, PASS_LEN), 1)
        tails.append(jnp.where(offsets < length, 0.0, LOWEST).astype(f32))
    starts = [at * PASS_LEN for at in starts]
    short_start = short_at * PASS_LEN
    kept = (n_pass - 1) * PASS_LEN + SHORT_LEN
    number = kept + SHORT_LEN

    own_queries.wait()
    view = query_buf.at[dec : 2 * dec]
    pltpu.make_async_copy(view, view, query_sem.at[1]).wait()

    heads = half // DK
    counted = jnp.concatenate(
        [jnp.ones((kept, DK), bf16), jnp.zeros((SHORT_LEN, DK), bf16)], axis=0
    )

    def head_cols(h):
        return slice(h * DK, (h + 1) * DK)

    def score(h, low, high):
        cols = head_cols(h)
        asked = jnp.concatenate([query_buf[low:high, cols], query_buf[dec + low : dec + high, cols]], axis=0)
        last = keys[pl.ds(short_start, SHORT_LEN), cols]
        against = jnp.concatenate(
            [keys[pl.ds(at, PASS_LEN), cols] for at in starts] + [last, last], axis=0
        )
        score_buf[h % 2] = lax.dot_general(
            asked, against, (((1,), (1,)), ((), ())), preferred_element_type=f32
        )

    def weigh(h, low, high):
        for row in range(0, 2 * (high - low), ROW_BLOCK):
            here = slice(row, row + ROW_BLOCK)
            scores = score_buf[h % 2, here, :]
            scores = jnp.concatenate(
                [scores[:, :PASS_LEN]]
                + [
                    scores[:, (j + 1) * PASS_LEN : (j + 2) * PASS_LEN] + tails[j]
                    for j in range(n_pass - 2)
                ]
                + [scores[:, (n_pass - 1) * PASS_LEN :]],
                axis=1,
            )
            top = jnp.max(scores, axis=-1, keepdims=True)
            weight_buf[h % 2, here, :] = jnp.exp(scores - top).astype(bf16)

    def mix(h, low, high):
        cols = head_cols(h)
        size = high - low
        taken = jnp.concatenate(
            [values[pl.ds(at, PASS_LEN), cols] for at in starts]
            + [values[pl.ds(short_start, SHORT_LEN), cols], jnp.zeros((SHORT_LEN, DK), bf16)],
            axis=0,
        )
        taken = jnp.concatenate([taken, counted], axis=1)
        mixed = jnp.dot(weight_buf[h % 2], taken, preferred_element_type=f32)
        mixed = (mixed[:, :DK] / mixed[:, DK:]).astype(bf16)
        attended[low:high, cols] = mixed[:size]
        attended[dec + low : dec + high, cols] = mixed[size:]

    def attend(low, high, hooks):
        for step in range(heads + 2):
            if step < heads:
                score(step, low, high)
            if 0 < step < heads + 1:
                weigh(step - 1, low, high)
            if 1 < step:
                mix(step - 2, low, high)
            if step in hooks:
                hooks[step]()

    chunks = width // OUT_CHUNK

    def chunk_of(j):
        return slice(j * OUT_CHUNK, (j + 1) * OUT_CHUNK)

    def to_core(n, low, high):
        here = slice(low, high)
        size = high - low
        mixed = jnp.concatenate([attended[low:high, :], attended[dec + low : dec + high, :]], axis=0)
        for j in range(chunks):
            cols = chunk_of(j)
            made = jnp.dot(mixed, out_w[:, cols], preferred_element_type=f32)
            core_send[here, cols] = made[size:].astype(bf16)
            send(
                core_send.at[here, cols], core_recv.at[here, cols], out_core_sem.at[0, n, j],
                out_core_sem.at[1, n, j], partner,
            )
            own_part[here, cols] = made[:size]

    def to_x(n, low, high):
        here = slice(low, high)
        for j in range(chunks):
            cols = chunk_of(j)
            view = core_recv.at[here, cols]
            pltpu.make_async_copy(view, view, out_core_sem.at[1, n, j]).wait()
            x_parts[x, here, cols] = (
                own_part[here, cols] + core_recv[here, cols].astype(f32)
            ).astype(bf16)
            view = x_parts.at[x, here, cols]
            for d, peer in enumerate(x_peers):
                send(view, view, out_x_sem.at[0, n, d, j], out_x_sem.at[1, n, d, j], peer)

    def finish(n, low, high):
        here = slice(low, high)
        for j in range(chunks):
            cols = chunk_of(j)
            for d in range(1, n_heads):
                view = x_parts.at[flip(x, d), here, cols]
                pltpu.make_async_copy(view, view, out_x_sem.at[1, n, d - 1, j]).wait()
            total = x_parts[0, here, cols].astype(f32)
            for term in range(1, n_heads):
                total += x_parts[term, here, cols].astype(f32)
            out_ref[here, cols] = total.astype(bf16)

    size = dec // SPLITS
    bounds = [(n * size, (n + 1) * size) for n in range(SPLITS)]
    for n, (low, high) in enumerate(bounds):
        hooks = {}
        if n:
            hooks[5] = functools.partial(to_x, n - 1, *bounds[n - 1])
        attend(low, high, hooks)
        if not n:
            for triple in loads:
                triple[2].wait()
        to_core(n, low, high)
    to_x(SPLITS - 1, *bounds[-1])
    for n, (low, high) in enumerate(bounds):
        finish(n, low, high)
    for copy in sent:
        copy.wait_send()


def on_device(
    n_rows, n_heads, queries, passages, enc_gain, key_weight, value_weight, out_weight, passage_length
):
    dec, inner = queries.shape
    block, width = passages.shape
    half = inner // 2
    n_pass = passage_length.shape[0]
    number = (n_pass - 1) * PASS_LEN + 2 * SHORT_LEN
    n_z = n_rows // 4
    slots = 2 * n_z
    chunks = width // OUT_CHUNK
    bf16 = jnp.bfloat16
    dma = pltpu.SemaphoreType.DMA
    vmem = pl.BlockSpec(memory_space=pltpu.VMEM)
    anywhere = pl.BlockSpec(memory_space=pl.ANY)
    n_sends = 2 * (n_z - 1) + 2 * n_z + 1 + (slots - 1) + 3 * (slots - 1)
    return pl.pallas_call(
        functools.partial(kernel, n_rows, n_heads),
        out_shape=jax.ShapeDtypeStruct((dec, width), bf16),
        in_specs=[
            anywhere,
            anywhere,
            anywhere,
            anywhere,
            anywhere,
            anywhere,
            anywhere,
        ],
        out_specs=vmem,
        scratch_shapes=[
            pltpu.SMEM((n_pass,), jnp.int32),
            pltpu.VMEM((width,), bf16),
            pltpu.VMEM((block, width), bf16),
            pltpu.VMEM((n_rows * block, width), bf16),
            pltpu.VMEM((2 * dec, half), bf16),
            pltpu.VMEM((width, half), bf16),
            pltpu.VMEM((width, half), bf16),
            pltpu.VMEM((half, width), bf16),
            pltpu.VMEM((n_rows * block, half), bf16),
            pltpu.VMEM((n_rows * block, half), bf16),
            pltpu.VMEM((2, (n_z - 1) * 2 * block, half), jnp.float32),
            pltpu.VMEM((2, (n_z - 1) * 2 * block, half), jnp.float32),
            pltpu.VMEM((2, 2 * dec // SPLITS, number), jnp.float32),
            pltpu.VMEM((2, 2 * dec // SPLITS, number), bf16),
            pltpu.VMEM((2 * dec, half), bf16),
            pltpu.VMEM((dec, width), bf16),
            pltpu.VMEM((dec, width), bf16),
            pltpu.VMEM((dec, width), jnp.float32),
            pltpu.VMEM((n_heads, dec, width), bf16),
            dma((4,)),
            dma((3, LOADS)),
            dma((n_sends,)),
            dma((slots, 2, 3)),
            dma((2,)),
            dma((2, SPLITS, chunks)),
            dma((2, SPLITS, n_heads - 1, chunks)),
        ],
        compiler_params=pltpu.CompilerParams(
            collective_id=0, has_side_effects=True, vmem_limit_bytes=40 * 1024 * 1024
        ),
    )(
        *(
            pltpu.with_memory_space_constraint(array, pltpu.HBM)
            for array in (
                passage_length,
                queries,
                passages,
                enc_gain,
                key_weight,
                value_weight,
                out_weight,
            )
        )
    )


def solution(mesh):
    return jax.shard_map(
        functools.partial(on_device, mesh.shape["rows"], mesh.shape["heads"]),
        mesh=mesh,
        in_specs=(
            P(("groups", "rows"), "heads"),
            P(("groups", "rows"), None),
            P(),
            P(None, "heads"),
            P(None, "heads"),
            P("heads", None),
            P("groups"),
        ),
        out_specs=P(("groups", "rows"), None),
        check_vma=False,
    )
```

```python
import functools

import jax
import jax.numpy as jnp
from jax import lax
from jax.experimental import pallas as pl
from jax.experimental.pallas import tpu as pltpu
from jax.sharding import PartitionSpec as P

DK = 128
PASS_LEN = 256
SHORT_LEN = PASS_LEN // 4
LOWEST = -1e30
MESH = pl.DeviceIdType.MESH
LOADS = 4
GROUP = 256
OUT_CHUNK = 512
ROW_BLOCK = 16
GIVE, SHARED, REST = 0, 1, 2
SPLITS = 2
PARTS = 2
EACH = 3


def flip(index, bits):
    bit = 1
    while bit <= bits:
        if bits & bit:
            index = index + bit - 2 * bit * ((index // bit) % 2)
        bit *= 2
    return index


def kernel(
    n_rows,
    n_heads,
    length_hbm,
    queries_ref,
    passages_ref,
    gain_hbm,
    key_ref,
    value_ref,
    outw_ref,
    out_ref,
    length_ref,
    gain_ref,
    own_raw,
    rows,
    query_buf,
    key_w,
    value_w,
    out_w,
    keys,
    values,
    key_sum,
    value_sum,
    score_buf,
    weight_buf,
    attended,
    core_send,
    core_recv,
    own_part,
    x_parts,
    local_sem,
    load_sem,
    send_sem,
    recv_sem,
    query_sem,
    out_core_sem,
    out_x_sem,
):
    block, width = passages_ref.shape
    dec, inner = queries_ref.shape
    half = inner // 2
    n_pass = length_ref.shape[0]
    n_z = n_rows // 4
    quarter = width // 4
    middle = width - 2 * quarter
    bf16 = jnp.bfloat16
    f32 = jnp.float32

    me = lax.axis_index("rows")
    x = lax.axis_index("heads")
    core = me % 2
    y = (me // 2) % 2
    z = me // 4
    side = x % 2

    def at_row(r):
        return {"rows": r}

    partner = at_row(flip(me, 1))
    across_y = at_row(flip(me, 2))
    z_peers = [at_row(flip(me, 4 * d)) for d in range(1, n_z)]
    x_peers = [{"heads": flip(x, d)} for d in range(1, n_heads)]
    across_x = x_peers[0]

    own_rows = pltpu.make_async_copy(passages_ref, own_raw, local_sem.at[0])
    own_rows.start()
    own_gain = pltpu.make_async_copy(gain_hbm, gain_ref, local_sem.at[2])
    own_gain.start()
    own_length = pltpu.make_async_copy(length_hbm, length_ref, local_sem.at[3])
    own_length.start()
    barrier = pltpu.get_barrier_semaphore()
    peers = z_peers + [across_y, partner] + x_peers
    for peer in peers:
        pl.semaphore_signal(barrier, inc=1, device_id=peer, device_id_type=MESH)

    mine = pl.ds(pl.multiple_of(core * half, 128), half)
    theirs = pl.ds(pl.multiple_of((1 - core) * half, 128), half)
    share = half // LOADS
    loads = []
    for part in range(LOADS):
        here = pl.ds(part * share, share)
        there = pl.ds(pl.multiple_of(core * half + part * share, 128), share)
        loads.append(
            (
                pltpu.make_async_copy(
                    key_ref.at[:, there], key_w.at[:, here], load_sem.at[0, part]
                ),
                pltpu.make_async_copy(
                    value_ref.at[:, there], value_w.at[:, here], load_sem.at[1, part]
                ),
                pltpu.make_async_copy(outw_ref.at[there], out_w.at[here], load_sem.at[2, part]),
            )
        )
    own_queries = pltpu.make_async_copy(
        queries_ref.at[:, mine], query_buf.at[0:dec], local_sem.at[1]
    )

    def slot_of(dy, dz):
        return dy * n_z + dz

    def place(slot, c):
        return pl.ds(pl.multiple_of(slot * 2 * block + c * block, 16), block)

    give_at = pl.multiple_of(side * (width - quarter), 128)
    rest_at = pl.multiple_of((1 - side) * (width - quarter), 128)
    rest_cols = pl.ds(rest_at, quarter)
    cols_of = {GIVE: pl.ds(give_at, quarter), SHARED: pl.ds(quarter, middle), REST: rest_cols}

    def unit_of(slot, c, kind):
        return rows.at[place(slot, c), cols_of[kind]]

    def whole_of(slot, c):
        return rows.at[place(slot, c)]

    own_rows.wait()
    own_gain.wait()
    for triple in loads:
        triple[0].start()
        triple[1].start()
    own_queries.start()
    for triple in loads:
        triple[2].start()
    wide_rows = own_raw[...].astype(f32)
    mean_square = jnp.mean(wide_rows * wide_rows, axis=-1, keepdims=True)
    gain = gain_ref[...].astype(f32).reshape(1, width)
    rows[place(0, core), :] = (wide_rows * lax.rsqrt(mean_square + 1e-06) * gain).astype(bf16)

    pl.semaphore_wait(barrier, len(peers))

    sent = []

    def send(src, dst, send_at, recv_at, to):
        copy = pltpu.make_async_remote_copy(
            src_ref=src, dst_ref=dst, send_sem=send_at, recv_sem=recv_at,
            device_id=to, device_id_type=MESH,
        )
        copy.start()
        sent.append(copy)

    count = [0]

    def next_sem():
        count[0] += 1
        return send_sem.at[count[0] - 1]

    def send_unit(slot, kind, to, there_slot, there_kind):
        send(
            unit_of(slot, core, kind),
            unit_of(there_slot, core, kind),
            next_sem(),
            recv_sem.at[there_slot, core, there_kind],
            to,
        )

    def await_unit(slot, c, kind):
        view = unit_of(slot, c, kind)
        pltpu.make_async_copy(view, view, recv_sem.at[slot, c, kind]).wait()

    def send_own(kind):
        for d in range(n_z - 1, 0, -1):
            send_unit(0, kind, z_peers[d - 1], slot_of(0, d), kind)
        if kind == GIVE:
            for early in (GIVE, SHARED):
                send_unit(0, early, across_y, slot_of(1, 0), early)

    send_own(GIVE)
    send(whole_of(0, core), whole_of(0, core), next_sem(), recv_sem.at[0, core, 0], partner)
    send(
        queries_ref.at[:, theirs], query_buf.at[dec : 2 * dec], query_sem.at[0], query_sem.at[1], partner
    )

    def relay(slot, kind, over_y):
        await_unit(slot, core, kind)
        if over_y:
            send_unit(slot, kind, across_y, slot + n_z, kind)
        if kind == GIVE:
            send_unit(slot, kind, across_x, slot, REST)
        send_unit(slot, kind, partner, slot, kind)

    groups = half // GROUP
    waited = set()

    def weights_for(g):
        part = g * GROUP // share
        if part not in waited:
            waited.add(part)
            loads[part][0].wait()
            loads[part][1].wait()

    def keep(slots, cols, made_keys, made_values):
        made_keys = made_keys.astype(bf16)
        made_values = made_values.astype(bf16)
        for number, slot in enumerate(slots):
            dy, dz = slot // n_z, slot % n_z
            chip = flip(z, dz) * 2 + flip(y, dy)
            to = pl.ds(pl.multiple_of(chip * 2 * block, 16), 2 * block)
            part = slice(number * 2 * block, (number + 1) * 2 * block)
            keys[to, cols] = made_keys[part]
            values[to, cols] = made_values[part]

    def rows_in(slots):
        return slice(slots[0] * 2 * block, (slots[-1] + 1) * 2 * block)

    def project(slots, g):
        weights_for(g)
        cols = slice(g * GROUP, (g + 1) * GROUP)
        chunk = rows[rows_in(slots), :]
        keep(
            slots,
            cols,
            jnp.dot(chunk, key_w[:, cols], preferred_element_type=f32),
            jnp.dot(chunk, value_w[:, cols], preferred_element_type=f32),
        )

    def project_part(which, cols_in, first, last, slots, g):
        cols = slice(g * GROUP, (g + 1) * GROUP)
        chunk = rows[rows_in(slots), cols_in]
        here = slice(0, len(slots) * 2 * block)
        made_keys = jnp.dot(chunk, key_w[cols_in, cols], preferred_element_type=f32)
        made_values = jnp.dot(chunk, value_w[cols_in, cols], preferred_element_type=f32)
        if not first:
            made_keys += key_sum[which, here, cols]
            made_values += value_sum[which, here, cols]
        if last:
            keep(slots, cols, made_keys, made_values)
        else:
            key_sum[which, here, cols] = made_keys
            value_sum[which, here, cols] = made_values

    def interleave(pieces, events, each):
        events = list(events)
        for piece in pieces:
            piece()
            for event in events[:each]:
                event()
            events = events[each:]
        for event in events:
            event()

    def pieces_of(work, slots, parts):
        def piece(part):
            for g in range(groups * part // parts, groups * (part + 1) // parts):
                work(slots, g)

        return [functools.partial(piece, part) for part in range(parts)]

    near = list(range(n_z - 1, 0, -1))
    line = [slot_of(0, d) for d in near]
    other = [slot_of(1, d) for d in near]
    beside = slot_of(1, 0)

    def from_partner(slots, kinds):
        for slot in slots:
            for kind in kinds:
                await_unit(slot, 1 - core, kind)

    R = functools.partial
    view = whole_of(0, 1 - core)
    pltpu.make_async_copy(view, view, recv_sem.at[0, 1 - core, 0]).wait()
    send_own(SHARED)
    interleave(pieces_of(project, [0], 1), [], 1)
    ahead, across = line[::-1], other[::-1]
    main_cols = pl.ds(pl.multiple_of(side * quarter, 128), width - quarter)
    late_cols = pl.ds(pl.multiple_of((1 - side) * quarter, 128), width - quarter)
    relay(beside, GIVE, False)
    for s in line:
        relay(s, GIVE, True)
    relay(beside, SHARED, False)
    from_partner(line, (GIVE,))
    interleave(pieces_of(R(project_part, 0, cols_of[GIVE], True, False), ahead, 1), [], 1)
    from_partner([beside], (GIVE, SHARED))
    interleave(pieces_of(R(project_part, 1, main_cols, True, False), [beside], 1), [], 1)
    for o in other:
        relay(o, GIVE, False)
    relay(beside, REST, False)
    for s in line:
        relay(s, SHARED, True)
    for s in line:
        relay(s, REST, False)
    from_partner([beside], (REST,))
    interleave(pieces_of(R(project_part, 1, cols_of[REST], False, True), [beside], 1), [], 1)
    from_partner(other, (GIVE,))
    interleave(pieces_of(R(project_part, 1, cols_of[GIVE], True, False), across, 1), [], 1)
    from_partner(line, (SHARED, REST))
    events = [R(relay, o, REST, False) for o in other]
    events += [R(relay, o, SHARED, False) for o in other]
    interleave(pieces_of(R(project_part, 0, late_cols, False, True), ahead, PARTS), events, EACH)
    from_partner(other, (REST,))
    interleave(pieces_of(R(project_part, 1, cols_of[REST], False, False), across, 1), [], 1)
    from_partner(other, (SHARED,))
    interleave(pieces_of(R(project_part, 1, cols_of[SHARED], False, True), across, 1), [], 1)

    own_length.wait()
    lengths = [length_ref[p] for p in range(n_pass)]
    short_at = jnp.int32(0)
    full_at = jnp.int32(0)
    short_open = jnp.int32(1)
    full_open = jnp.int32(1)
    for p in range(n_pass):
        hit = short_open * (lengths[p] == SHORT_LEN).astype(jnp.int32)
        short_at = short_at + hit * p
        short_open = short_open - hit
        hit = full_open * (lengths[p] == PASS_LEN).astype(jnp.int32)
        full_at = full_at + hit * p
        full_open = full_open - hit
    starts = [full_at]
    tails = []
    for j in range(n_pass - 2):
        low = short_at + (full_at < short_at).astype(jnp.int32) * (full_at - short_at)
        high = short_at + full_at - low
        at = j + (j >= low).astype(jnp.int32)
        at = at + (at >= high).astype(jnp.int32)
        starts.append(at)
        length = jnp.int32(0)
        for p in range(n_pass):
            length = length + (at == p).astype(jnp.int32) * lengths[p]
        offsets = lax.broadcasted_iota(jnp.int32, (1, PASS_LEN), 1)
        tails.append(jnp.where(offsets < length, 0.0, LOWEST).astype(f32))
    starts = [at * PASS_LEN for at in starts]
    short_start = short_at * PASS_LEN
    kept = (n_pass - 1) * PASS_LEN + SHORT_LEN
    number = kept + SHORT_LEN

    own_queries.wait()
    view = query_buf.at[dec : 2 * dec]
    pltpu.make_async_copy(view, view, query_sem.at[1]).wait()

    heads = half // DK
    counted = jnp.concatenate(
        [jnp.ones((kept, DK), bf16), jnp.zeros((SHORT_LEN, DK), bf16)], axis=0
    )

    def head_cols(h):
        return slice(h * DK, (h + 1) * DK)

    def score(h, low, high):
        cols = head_cols(h)
        asked = jnp.concatenate([query_buf[low:high, cols], query_buf[dec + low : dec + high, cols]], axis=0)
        last = keys[pl.ds(short_start, SHORT_LEN), cols]
        against = jnp.concatenate(
            [keys[pl.ds(at, PASS_LEN), cols] for at in starts] + [last, last], axis=0
        )
        score_buf[h % 2] = lax.dot_general(
            asked, against, (((1,), (1,)), ((), ())), preferred_element_type=f32
        )

    def weigh(h, low, high):
        for row in range(0, 2 * (high - low), ROW_BLOCK):
            here = slice(row, row + ROW_BLOCK)
            scores = score_buf[h % 2, here, :]
            scores = jnp.concatenate(
                [scores[:, :PASS_LEN]]
                + [
                    scores[:, (j + 1) * PASS_LEN : (j + 2) * PASS_LEN] + tails[j]
                    for j in range(n_pass - 2)
                ]
                + [scores[:, (n_pass - 1) * PASS_LEN :]],
                axis=1,
            )
            top = jnp.max(scores, axis=-1, keepdims=True)
            weight_buf[h % 2, here, :] = jnp.exp(scores - top).astype(bf16)

    def mix(h, low, high):
        cols = head_cols(h)
        size = high - low
        taken = jnp.concatenate(
            [values[pl.ds(at, PASS_LEN), cols] for at in starts]
            + [values[pl.ds(short_start, SHORT_LEN), cols], jnp.zeros((SHORT_LEN, DK), bf16)],
            axis=0,
        )
        taken = jnp.concatenate([taken, counted], axis=1)
        mixed = jnp.dot(weight_buf[h % 2], taken, preferred_element_type=f32)
        mixed = (mixed[:, :DK] / mixed[:, DK:]).astype(bf16)
        attended[low:high, cols] = mixed[:size]
        attended[dec + low : dec + high, cols] = mixed[size:]

    def attend(low, high, hooks):
        for step in range(heads + 2):
            if step < heads:
                score(step, low, high)
            if 0 < step < heads + 1:
                weigh(step - 1, low, high)
            if 1 < step:
                mix(step - 2, low, high)
            if step in hooks:
                hooks[step]()

    chunks = width // OUT_CHUNK

    def chunk_of(j):
        return slice(j * OUT_CHUNK, (j + 1) * OUT_CHUNK)

    def to_core(n, low, high):
        here = slice(low, high)
        size = high - low
        mixed = jnp.concatenate([attended[low:high, :], attended[dec + low : dec + high, :]], axis=0)
        for j in range(chunks):
            cols = chunk_of(j)
            made = jnp.dot(mixed, out_w[:, cols], preferred_element_type=f32)
            core_send[here, cols] = made[size:].astype(bf16)
            send(
                core_send.at[here, cols], core_recv.at[here, cols], out_core_sem.at[0, n, j],
                out_core_sem.at[1, n, j], partner,
            )
            own_part[here, cols] = made[:size]

    def to_x(n, low, high):
        here = slice(low, high)
        for j in range(chunks):
            cols = chunk_of(j)
            view = core_recv.at[here, cols]
            pltpu.make_async_copy(view, view, out_core_sem.at[1, n, j]).wait()
            x_parts[x, here, cols] = (
                own_part[here, cols] + core_recv[here, cols].astype(f32)
            ).astype(bf16)
            view = x_parts.at[x, here, cols]
            for d, peer in enumerate(x_peers):
                send(view, view, out_x_sem.at[0, n, d, j], out_x_sem.at[1, n, d, j], peer)

    def finish(n, low, high):
        here = slice(low, high)
        for j in range(chunks):
            cols = chunk_of(j)
            for d in range(1, n_heads):
                view = x_parts.at[flip(x, d), here, cols]
                pltpu.make_async_copy(view, view, out_x_sem.at[1, n, d - 1, j]).wait()
            total = x_parts[0, here, cols].astype(f32)
            for term in range(1, n_heads):
                total += x_parts[term, here, cols].astype(f32)
            out_ref[here, cols] = total.astype(bf16)

    size = dec // SPLITS
    bounds = [(n * size, (n + 1) * size) for n in range(SPLITS)]
    for n, (low, high) in enumerate(bounds):
        hooks = {}
        if n:
            hooks[5] = functools.partial(to_x, n - 1, *bounds[n - 1])
        attend(low, high, hooks)
        if not n:
            for triple in loads:
                triple[2].wait()
        to_core(n, low, high)
    to_x(SPLITS - 1, *bounds[-1])
    for n, (low, high) in enumerate(bounds):
        finish(n, low, high)
    for copy in sent:
        copy.wait_send()


def on_device(
    n_rows, n_heads, queries, passages, enc_gain, key_weight, value_weight, out_weight, passage_length
):
    dec, inner = queries.shape
    block, width = passages.shape
    half = inner // 2
    n_pass = passage_length.shape[0]
    number = (n_pass - 1) * PASS_LEN + 2 * SHORT_LEN
    n_z = n_rows // 4
    slots = 2 * n_z
    chunks = width // OUT_CHUNK
    bf16 = jnp.bfloat16
    dma = pltpu.SemaphoreType.DMA
    vmem = pl.BlockSpec(memory_space=pltpu.VMEM)
    anywhere = pl.BlockSpec(memory_space=pl.ANY)
    n_sends = 2 * (n_z - 1) + 2 * n_z + 1 + (slots - 1) + 3 * (slots - 1)
    return pl.pallas_call(
        functools.partial(kernel, n_rows, n_heads),
        out_shape=jax.ShapeDtypeStruct((dec, width), bf16),
        in_specs=[
            anywhere,
            anywhere,
            anywhere,
            anywhere,
            anywhere,
            anywhere,
            anywhere,
        ],
        out_specs=vmem,
        scratch_shapes=[
            pltpu.SMEM((n_pass,), jnp.int32),
            pltpu.VMEM((width,), bf16),
            pltpu.VMEM((block, width), bf16),
            pltpu.VMEM((n_rows * block, width), bf16),
            pltpu.VMEM((2 * dec, half), bf16),
            pltpu.VMEM((width, half), bf16),
            pltpu.VMEM((width, half), bf16),
            pltpu.VMEM((half, width), bf16),
            pltpu.VMEM((n_rows * block, half), bf16),
            pltpu.VMEM((n_rows * block, half), bf16),
            pltpu.VMEM((2, (n_z - 1) * 2 * block, half), jnp.float32),
            pltpu.VMEM((2, (n_z - 1) * 2 * block, half), jnp.float32),
            pltpu.VMEM((2, 2 * dec // SPLITS, number), jnp.float32),
            pltpu.VMEM((2, 2 * dec // SPLITS, number), bf16),
            pltpu.VMEM((2 * dec, half), bf16),
            pltpu.VMEM((dec, width), bf16),
            pltpu.VMEM((dec, width), bf16),
            pltpu.VMEM((dec, width), jnp.float32),
            pltpu.VMEM((n_heads, dec, width), bf16),
            dma((4,)),
            dma((3, LOADS)),
            dma((n_sends,)),
            dma((slots, 2, 3)),
            dma((2,)),
            dma((2, SPLITS, chunks)),
            dma((2, SPLITS, n_heads - 1, chunks)),
        ],
        compiler_params=pltpu.CompilerParams(
            collective_id=0, has_side_effects=True, vmem_limit_bytes=40 * 1024 * 1024
        ),
    )(
        *(
            pltpu.with_memory_space_constraint(array, pltpu.HBM)
            for array in (
                passage_length,
                queries,
                passages,
                enc_gain,
                key_weight,
                value_weight,
                out_weight,
            )
        )
    )


def solution(mesh):
    return jax.shard_map(
        functools.partial(on_device, mesh.shape["rows"], mesh.shape["heads"]),
        mesh=mesh,
        in_specs=(
            P(("groups", "rows"), "heads"),
            P(("groups", "rows"), None),
            P(),
            P(None, "heads"),
            P(None, "heads"),
            P("heads", None),
            P("groups"),
        ),
        out_specs=P(("groups", "rows"), None),
        check_vma=False,
    )
```
